512 devices in a mesh: pb: 64 (over z_lo, x, core), wa: 8 (over y, z_hi).
Axes of the slice: x: 4, y: 4, z: 16 (z_hi: 2, z_lo: 8; z = z_hi * 8 + z_lo), core: 2. Of those that a mesh axis runs over, the one named last changes fastest.
Arguments:
- psi_val: bfloat16 [16, 8, 1024], P('wa', None, 'pb'), may hold values from -0.796875 to 0.796875
- psi_cond: bfloat16 [16, 12, 1024], P('wa', None, 'pb'), may hold values from -0.796875 to 0.796875
- trials: bfloat16 [16, 1536], P('wa', 'pb'), may hold values from -6 to 6
- screened: bfloat16 [64, 1024, 1024], P('pb', 'wa'), may hold values from -0.1875 to 0.1875
- kmap: int32 [64, 16], P('pb'), may hold values from 0 to 15, each once within a row
Outputs:
- action: float32 [16, 1536], P('wa', 'pb')
The draws below stay inside these ranges and needn't reach their ends.
Inputs may be any that keep to these rules, and one draw needn't show every extreme that they name: Every row of kmap is a permutation of the 16 k-points.
All inputs are finite; a program needn't handle non-finite values.
Results may differ from the reference program's by a relative error of at most 0.005.
Values may be sent and summed in bfloat16 or wider, within the bound.
No kernel may reach another device: no remote copies, remote signals or barrier semaphores. Data moves between devices by JAX's collectives and lax.ppermute only.
A program may use at most 64 MiB of HBM per device.

```python
import jax
import jax.numpy as jnp
from jax import lax

V = 8
C = 12
MU = 1024
K = 16
S = 16
Q = 64


def level_of(stream_key, shape, split, smallest, top_value):
    loudness = 1.0
    for position, shards_of in split:
        steps = jax.random.uniform(jax.random.fold_in(jax.random.fold_in(stream_key, 6), position), (shards_of,), jnp.float32, smallest / len(split), top_value / len(split))
        loudness = loudness * jnp.repeat(jnp.exp(steps), shape[position] // shards_of).reshape((-1,) + (1,) * (len(shape) - 1 - position))
    return loudness


def gaussian(key, dims, scale, bound, shards=(), held_as=jnp.bfloat16):
    values = scale * jax.random.normal(key, dims, jnp.float32)
    if shards:
        values = values * level_of(key, dims, shards, -0.22, 0.18)
    return jnp.clip(values, -bound, bound).astype(held_as)


def setup_inputs(seed: int = 0) -> dict:
    streams_of = jax.random.split(jax.random.key(seed), 6)
    psi_val = gaussian(streams_of[0], (K, V, MU), 0.13, 0.796875, ((0, 8), (2, 64)))
    psi_cond = gaussian(streams_of[1], (K, C, MU), 0.13, 0.796875, ((0, 8), (2, 64)))
    trials = gaussian(streams_of[2], (K, S * V * C), 1.0, 6.0, ((0, 8), (1, 64)))
    screened = gaussian(streams_of[3], (Q, MU, MU), MU ** -0.5, 0.1875, ((0, 64), (1, 8)))
    kmap = jax.vmap(lambda own: jax.random.permutation(own, K))(jax.random.split(streams_of[4], Q)).reshape((Q, K)).astype(jnp.int32)
    return dict(psi_val=psi_val, psi_cond=psi_cond, trials=trials, screened=screened, kmap=kmap)


def one_transfer(psi_val, psi_cond, xfull, wq, row):
    hi = lax.Precision.HIGHEST
    valf = psi_val.astype(jnp.float32)
    condf = psi_cond.astype(jnp.float32)
    valp = valf[row]
    condp = condf[row]
    apair = (valf[:, :, None, :] * valp[:, None, :, :]).astype(jnp.bfloat16)
    bpair = (condf[:, :, None, :] * condp[:, None, :, :]).astype(jnp.bfloat16)
    wfull = wq.astype(jnp.float32)
    wa_term = jnp.dot(apair.reshape(-1, MU).astype(jnp.float32), wfull.T, precision=hi).astype(jnp.bfloat16)
    wb_term = jnp.dot(bpair.reshape(-1, MU).astype(jnp.float32), wfull.T, precision=hi).astype(jnp.bfloat16)
    wa_term = wa_term.reshape(K, V, V, MU).astype(jnp.float32)
    wb_term = wb_term.reshape(K, C, C, MU).astype(jnp.float32)
    gmat = jnp.einsum('kcdm,kvum->kcdvu', bpair.astype(jnp.float32), wa_term, precision=hi)
    hmat = jnp.einsum('kcdm,kvum->kcdvu', wb_term, apair.astype(jnp.float32), precision=hi)
    forward = jnp.einsum('kcdvu,ksud->ksvc', gmat, xfull[row], precision=hi)
    backward = jnp.einsum('kdcuv,ksud->ksvc', hmat, xfull, precision=hi)
    return forward + jnp.zeros((K, S, V, C), jnp.float32).at[row].add(backward)


def reference(psi_val, psi_cond, trials, screened, kmap):
    xfull = trials.astype(jnp.float32).reshape(K, S, V, C)

    def step(total, pieces):
        wq, row = pieces
        return total + one_transfer(psi_val, psi_cond, xfull, wq, row.astype(jnp.int32)), None

    total, unused = lax.scan(step, jnp.zeros((K, S, V, C), jnp.float32), (screened, kmap))
    return total.reshape(K, S * V * C)
```

```python
import itertools

import jax
import jax.numpy as jnp
from jax import lax
from jax.experimental import pallas as pl
from jax.experimental.pallas import tpu as pltpu
from jax.sharding import PartitionSpec as P

AXES = ("pb", "wa")
NX, NY, NZ, NC = 4, 4, 16, 2
F32 = jnp.float32
BF16 = jnp.bfloat16


def place(x, y, z, c):
    return (((z % 8) * NX + x) * NC + c) * 8 + y * 2 + z // 8


def lines():
    spans = itertools.product(range(NX), range(NY), range(NC))
    return [[place(x, y, z, c) for z in range(NZ)] for x, y, c in spans]


def planes():
    spots = list(itertools.product(range(NY), range(NX), range(NC)))
    return [[place(x, y, z, c) for y, x, c in spots] for z in range(NZ)]


def swap_kernel(in_ref, out_ref, wide):
    wide[...] = in_ref[...].astype(F32).reshape(128, 128)
    row = lax.broadcasted_iota(jnp.int32, (8, 128), 0)
    lane = lax.broadcasted_iota(jnp.int32, (8, 128), 1) // 16
    turn = lax.rem(row - lane + 8, 8)
    tiles = []
    for zh in range(2):
        for a in range(6):
            tile = wide[pl.ds(zh * 64 + a, 8, stride=8), :]
            done = jnp.where(turn == 0, tile, 0.0)
            for step in range(1, 8):
                moved = pltpu.roll(pltpu.roll(tile, step, 0), 128 - 16 * step, 1)
                done = jnp.where(turn == step, moved, done)
            tiles.append(done)
    block = jnp.concatenate(tiles, axis=0).astype(BF16)
    for dest in range(out_ref.shape[0]):
        out_ref[dest] = block


def swap(x):
    return pl.pallas_call(
        swap_kernel,
        out_shape=jax.ShapeDtypeStruct((32, 96, 128), BF16),
        in_specs=[pl.BlockSpec(memory_space=pltpu.VMEM)],
        out_specs=pl.BlockSpec(memory_space=pltpu.VMEM),
        scratch_shapes=[pltpu.VMEM((128, 128), F32)],
        name="swap",
    )(x)


NT = (((1,), (1,)), ((), ()))


def main_kernel(
    kmap_ref, spot_ref, r_ref, w_ref, o_ref, wt, psi, loc, t1, t2, ww, lf, acc, back
):
    spot = spot_ref[0]
    lane16 = lax.broadcasted_iota(jnp.int32, (8, 128), 1) // 16
    sub8 = lax.broadcasted_iota(jnp.int32, (8, 128), 0)
    own = lane16 == sub8

    for z in range(8):
        turned = w_ref[:, z * 128 : (z + 1) * 128].astype(F32).T.astype(BF16)
        for xc in range(8):
            wt[xc * 128 + z * 16 : xc * 128 + (z + 1) * 16, :] = turned[
                xc * 16 : (xc + 1) * 16
            ]
    acc[...] = jnp.zeros_like(acc)
    back[...] = jnp.zeros_like(back)

    lane24 = lax.broadcasted_iota(jnp.int32, (24, 128), 1) // 16

    def spread(k, carry):
        y, k4 = k // 4, lax.rem(k, 4)
        local = jnp.zeros((24, 128), F32)
        for xc in range(8):
            tile = r_ref[y, xc, k4].astype(F32)
            psi[k, :, xc * 128 : (xc + 1) * 128] = tile
            shift = lax.rem((xc - spot + 8) * 16, 128)
            local = jnp.where(lane24 == xc, pltpu.roll(tile, shift, 1), local)
        loc[k] = local
        rows, cols = [], []
        for u in range(8):
            for xh in range(2):
                xc = xh * 4 + u // 2
                at = psi[k, 20 + u % 2 : 21 + u % 2, xc * 128 : (xc + 1) * 128]
                rows.append(jnp.where(own, jnp.broadcast_to(at, (8, 128)), 0.0))
        left = jnp.concatenate(rows, axis=0).astype(BF16)
        right = jnp.concatenate([local[8:24]] * 8, axis=0).astype(BF16)
        t1[k] = jnp.dot(left, right, preferred_element_type=F32)
        for xh in range(2):
            x8 = jnp.concatenate(
                [
                    psi[k, 20:22, (xh * 4 + i) * 128 : (xh * 4 + i + 1) * 128]
                    for i in range(4)
                ],
                axis=0,
            )
            t2[k, xh] = jnp.dot(
                x8.T.astype(BF16), local[0:8].astype(BF16), preferred_element_type=F32
            )
        return carry

    lax.fori_loop(0, 16, spread, 0)

    def pair(k, carry):
        p = kmap_ref[k]
        val_here = psi[k, 0:8, :]
        cond_there = psi[p, 8:24, :]
        parts = [psi[p, u : u + 1, :] * val_here for u in range(8)]
        parts += [psi[k, 8 + d : 9 + d, :] * cond_there for d in range(12)]
        pairs = jnp.concatenate([part.astype(BF16) for part in parts], axis=0)
        ww[...] = jnp.dot(pairs, wt[...], preferred_element_type=F32)

        left = jnp.concatenate(
            [ww[u * 8 : (u + 1) * 8, :].astype(BF16) for u in range(8)], axis=1
        )
        for xh in range(2):
            for u in range(8):
                tile = t1[p, (u * 2 + xh) * 8 : (u * 2 + xh + 1) * 8, :]
                grown = [
                    tile * jnp.broadcast_to(loc[k, 8 + c : 9 + c, :], (8, 128))
                    for c in range(12)
                ]
                lf[:, u * 128 : (u + 1) * 128] = jnp.concatenate(grown, axis=0).astype(
                    BF16
                )
            base = (k * 2 + xh) * 8
            acc[pl.ds(pl.multiple_of(base, 8), 8), 0:96] = lax.dot_general(
                left, lf[...], NT, preferred_element_type=F32
            )
        val_there = loc[p, 0:8, :].astype(BF16)
        for xh in range(2):
            cols = [t2[k, xh, pl.ds(d, 8, stride=16), :] for d in range(12)]
            sums = []
            for c in range(12):
                total = cols[0] * jnp.broadcast_to(ww[64 + c : 65 + c, :], (8, 128))
                for d in range(1, 12):
                    at = 64 + d * 16 + c
                    total += cols[d] * jnp.broadcast_to(ww[at : at + 1, :], (8, 128))
                sums.append(total)
            right = jnp.concatenate(sums, axis=0).astype(BF16)
            base = (p * 2 + xh) * 8
            back[pl.ds(pl.multiple_of(base, 8), 8), 0:96] = lax.dot_general(
                val_there, right, NT, preferred_element_type=F32
            )
        return carry

    lax.fori_loop(0, 16, pair, 0)

    acc[...] += back[...]
    for y in range(4):
        for xc in range(8):
            for ih in range(2):
                at = (y * 8 + xc // 4) * 8 + (xc % 4) * 2 + ih
                o_ref[y * 8 + xc, ih * 4 : (ih + 1) * 4, :] = acc[
                    pl.ds(at, 4, stride=16), :
                ]


def main(pairing, spot, gathered, weights):
    vmem = pl.BlockSpec(memory_space=pltpu.VMEM)
    smem = pl.BlockSpec(memory_space=pltpu.SMEM)
    return pl.pallas_call(
        main_kernel,
        out_shape=jax.ShapeDtypeStruct((32, 8, 128), F32),
        in_specs=[smem, smem, vmem, vmem],
        out_specs=vmem,
        scratch_shapes=[
            pltpu.VMEM((1024, 128), BF16),
            pltpu.VMEM((16, 24, 1024), F32),
            pltpu.VMEM((16, 24, 128), F32),
            pltpu.VMEM((16, 128, 128), F32),
            pltpu.VMEM((16, 2, 128, 128), F32),
            pltpu.VMEM((256, 128), F32),
            pltpu.VMEM((96, 1024), BF16),
            pltpu.VMEM((256, 128), F32),
            pltpu.VMEM((256, 128), F32),
        ],
        name="act",
    )(pairing, spot, gathered, weights)


def shards(psi_val, psi_cond, trials, screened, kmap):
    extra = jnp.pad(trials.reshape(2, 2, 12), ((0, 0), (0, 2), (0, 4)))
    line = jnp.concatenate([psi_val, psi_cond, extra], axis=1).reshape(6, 128)
    line = jnp.pad(line, ((0, 2), (0, 0)))
    along = lax.all_to_all(
        jnp.broadcast_to(line, (16, 8, 128)),
        AXES,
        0,
        0,
        tiled=True,
        axis_index_groups=lines(),
    )
    across = lax.all_to_all(
        swap(along), AXES, 0, 0, tiled=True, axis_index_groups=planes()
    )
    spot = lax.axis_index("wa").reshape(1)
    sums = main(
        kmap.reshape(16), spot, across.reshape(4, 8, 4, 24, 128), screened[0]
    )
    sums = lax.all_to_all(sums, AXES, 0, 0, tiled=True, axis_index_groups=planes())
    sums = jnp.sum(sums, axis=0)[:, :96].reshape(2, 2, 2, 12, 8)
    sums = sums.transpose(1, 4, 2, 0, 3).reshape(16, 48)
    sums = lax.all_to_all(sums, AXES, 0, 0, tiled=True, axis_index_groups=lines())
    return jnp.sum(sums, axis=0).reshape(2, 24)


def solution(mesh):
    in_specs = (
        P("wa", None, "pb"),
        P("wa", None, "pb"),
        P("wa", "pb"),
        P("pb", "wa", None),
        P("pb", None),
    )
    return jax.shard_map(
        shards, mesh=mesh, in_specs=in_specs, out_specs=P("wa", "pb"), check_vma=False
    )
```

```python
import itertools

import jax
import jax.numpy as jnp
from jax import lax
from jax.experimental import pallas as pl
from jax.experimental.pallas import tpu as pltpu
from jax.sharding import PartitionSpec as P

AXES = ("pb", "wa")
NX, NY, NZ, NC = 4, 4, 16, 2
F32 = jnp.float32
BF16 = jnp.bfloat16
NT = (((1,), (1,)), ((), ()))


def place(x, y, z, c):
    return (((z % 8) * NX + x) * NC + c) * 8 + y * 2 + z // 8


def lines():
    spans = itertools.product(range(NX), range(NY), range(NC))
    return [[place(x, y, z, c) for z in range(NZ)] for x, y, c in spans]


def planes():
    spots = list(itertools.product(range(NY), range(NX), range(NC)))
    return [[place(x, y, z, c) for y, x, c in spots] for z in range(NZ)]


def sheets():
    spots = list(itertools.product(range(NY), range(NX)))
    spans = itertools.product(range(NZ), range(NC))
    return [[place(x, y, z, c) for y, x in spots] for z, c in spans]


def partners():
    return [(i, i ^ 8) for i in range(NX * NY * NZ * NC)]


def exchange(x, groups):
    return lax.all_to_all(x, AXES, 0, 0, tiled=True, axis_index_groups=groups)


def swap_kernel(in_ref, out_ref, wide):
    wide[...] = in_ref[...].astype(F32).reshape(128, 128)
    row = lax.broadcasted_iota(jnp.int32, (8, 128), 0)
    lane = lax.broadcasted_iota(jnp.int32, (8, 128), 1) // 16
    turn = lax.rem(row - lane + 8, 8)
    tiles = []
    for zh in range(2):
        for a in range(6):
            tile = wide[pl.ds(zh * 64 + a, 8, stride=8), :]
            done = jnp.where(turn == 0, tile, 0.0)
            for step in range(1, 8):
                moved = pltpu.roll(pltpu.roll(tile, step, 0), 128 - 16 * step, 1)
                done = jnp.where(turn == step, moved, done)
            tiles.append(done)
    block = jnp.concatenate(tiles, axis=0).astype(BF16)
    for dest in range(out_ref.shape[0]):
        out_ref[dest] = block


def swap(x):
    vmem = pl.BlockSpec(memory_space=pltpu.VMEM)
    return pl.pallas_call(
        swap_kernel,
        out_shape=jax.ShapeDtypeStruct((NX * NY, 96, 128), BF16),
        in_specs=[vmem],
        out_specs=vmem,
        scratch_shapes=[pltpu.VMEM((128, 128), F32)],
        compiler_params=pltpu.CompilerParams(vmem_limit_bytes=4 << 20),
        name="swap",
    )(x)


def main_kernel(
    kmap_ref, spot_ref, own_ref, other_ref, w_ref, o_ref,
    wt, psi, half, loc, t1, t2, mixed, wa, wb, acc, back,
):
    spot, core = spot_ref[0], spot_ref[1]
    lane16 = lax.broadcasted_iota(jnp.int32, (8, 128), 1) // 16
    own_row = lane16 == lax.broadcasted_iota(jnp.int32, (8, 128), 0)
    lane24 = lax.broadcasted_iota(jnp.int32, (24, 128), 1) // 16

    for z in range(8):
        turned = w_ref[:, z * 128 : (z + 1) * 128].astype(F32).T.astype(BF16)
        for xc in range(8):
            wt[xc * 128 + z * 16 : xc * 128 + (z + 1) * 16, :] = turned[
                xc * 16 : (xc + 1) * 16
            ]

    def spread_one(k, j):
        y, k4 = k // 4, lax.rem(k, 4)
        local = jnp.zeros((24, 128), F32)
        for x in range(4):
            for ref, c in ((own_ref, core), (other_ref, 1 - core)):
                xc = x * 2 + c
                tile16 = ref[y, x, k4]
                tile = tile16.astype(F32)
                lanes = pl.ds(pl.multiple_of(xc * 128, 128), 128)
                psi[k, :, lanes] = tile
                half[k, :, lanes] = tile16
                shift = lax.rem((xc - spot + 8) * 16, 128)
                local = jnp.where(lane24 == xc, pltpu.roll(tile, shift, 1), local)
        loc[k] = local
        rows, flat = [], []
        for u in range(8):
            for xh in range(2):
                xc = xh * 4 + u // 2
                at = psi[k, 12 + u % 2 : 13 + u % 2, xc * 128 : (xc + 1) * 128]
                rows.append(jnp.where(own_row, jnp.broadcast_to(at, (8, 128)), 0.0))
        left = jnp.concatenate(rows, axis=0).astype(BF16)
        right = jnp.concatenate([local[0:16].astype(BF16)] * 8, axis=0)
        first = jnp.dot(left, right, preferred_element_type=F32).astype(BF16)
        for u in range(8):
            t1[k, :, u * 128 : (u + 1) * 128] = first[u * 16 : (u + 1) * 16]
        flat = jnp.concatenate(
            [psi[k, 12:14, xc * 128 : (xc + 1) * 128] for xc in range(8)], axis=0
        )
        val = local[16:24].astype(BF16)
        none = jnp.zeros_like(val)
        right = jnp.concatenate(
            [
                jnp.concatenate([val, none], axis=1),
                jnp.concatenate([none, val], axis=1),
            ],
            axis=0,
        )
        second = jnp.dot(flat.T.astype(BF16), right, preferred_element_type=F32)
        for xh in range(2):
            mixed[j, xh] = second[:, xh * 128 : (xh + 1) * 128]
        for d in range(12):
            both = [mixed[j, xh, pl.ds(d, 8, stride=16), :] for xh in range(2)]
            t2[k, :, d * 128 : (d + 1) * 128] = jnp.concatenate(both, axis=0).astype(BF16)

    def spread(i, carry):
        for j in range(2):
            spread_one(i * 2 + j, j)
        return carry

    lax.fori_loop(0, 8, spread, 0)

    def grown(row):
        return jnp.broadcast_to(row, (16, row.shape[1])).astype(BF16)

    def pairs_of(k, j):
        p = kmap_ref[k]
        val_here = half[k, 16:24, :]
        val_here = jnp.concatenate([val_here, val_here], axis=0)
        cond_there = half[p, 0:16, :]
        parts = []
        for u in range(0, 8, 2):
            two = [
                jnp.broadcast_to(psi[p, 16 + u + i : 17 + u + i, :], (8, 1024))
                for i in range(2)
            ]
            parts.append(jnp.concatenate(two, axis=0).astype(BF16) * val_here)
        for d in range(12):
            parts.append(grown(psi[k, d : d + 1, :]) * cond_there)
        ww = jnp.dot(
            jnp.concatenate(parts, axis=0), wt[...], preferred_element_type=F32
        )
        wa[j] = ww[0:64]
        wb[j] = ww[64:256].astype(BF16)

    def close(k, j):
        p = kmap_ref[k]
        cond = loc[k, 0:16, :].astype(BF16)
        vals = [grown(loc[p, 16 + v : 17 + v, :]) for v in range(8)]
        lf = jnp.concatenate(
            [
                jnp.concatenate(
                    [grown(wa[j, u * 8 + v : u * 8 + v + 1, :]) * cond for v in range(8)],
                    axis=0,
                )
                for u in range(8)
            ],
            axis=1,
        )
        lb = jnp.concatenate(
            [
                jnp.concatenate(
                    [wb[j, d * 16 : (d + 1) * 16] * vals[v] for v in range(8)], axis=0
                )
                for d in range(12)
            ],
            axis=1,
        )
        acc[k] = lax.dot_general(t1[p], lf, NT, preferred_element_type=F32)
        back[p] = lax.dot_general(t2[k], lb, NT, preferred_element_type=F32)

    pairs_of(0, 0)

    def pair(i, carry):
        k = i * 2
        pairs_of(k + 1, 1)
        close(k, 0)
        pairs_of(lax.rem(k + 2, 16), 0)
        close(k + 1, 1)
        return carry

    lax.fori_loop(0, 8, pair, 0)

    lane32 = lax.broadcasted_iota(jnp.int32, (8, 128), 1) // 32
    for y in range(4):
        for xh in range(2):
            rows = slice(xh * 8, (xh + 1) * 8)
            held = [acc[y * 4 + i, rows] + back[y * 4 + i, rows] for i in range(4)]
            for vv in range(4):
                done = held[vv]
                for k4 in range(4):
                    if k4 != vv:
                        moved = pltpu.roll(held[k4], (k4 - vv) * 32 % 128, 1)
                        done = jnp.where(lane32 == k4, moved, done)
                o_ref[y * 8 + xh * 4 + vv] = done


def main(pairing, spot, own, other, weights):
    vmem = pl.BlockSpec(memory_space=pltpu.VMEM)
    smem = pl.BlockSpec(memory_space=pltpu.SMEM)
    return pl.pallas_call(
        main_kernel,
        out_shape=jax.ShapeDtypeStruct((32, 8, 128), F32),
        in_specs=[smem, smem, vmem, vmem, vmem],
        out_specs=vmem,
        scratch_shapes=[
            pltpu.VMEM((1024, 128), BF16),
            pltpu.VMEM((16, 24, 1024), F32),
            pltpu.VMEM((16, 24, 1024), BF16),
            pltpu.VMEM((16, 24, 128), F32),
            pltpu.VMEM((16, 16, 1024), BF16),
            pltpu.VMEM((16, 16, 1536), BF16),
            pltpu.VMEM((2, 2, 128, 128), F32),
            pltpu.VMEM((2, 64, 128), F32),
            pltpu.VMEM((2, 192, 128), BF16),
            pltpu.VMEM((16, 16, 128), F32),
            pltpu.VMEM((16, 16, 128), F32),
        ],
        compiler_params=pltpu.CompilerParams(vmem_limit_bytes=16 << 20),
        name="act",
    )(pairing, spot, own, other, weights)


def shards(psi_val, psi_cond, trials, screened, kmap):
    extra = jnp.pad(trials.reshape(2, 2, 12), ((0, 0), (0, 2), (0, 4)))
    line = jnp.concatenate([psi_cond, extra, psi_val], axis=1).reshape(6, 128)
    line = jnp.pad(line, ((0, 2), (0, 0)))
    along = exchange(jnp.broadcast_to(line, (16, 8, 128)), lines())
    own = exchange(swap(along), sheets())
    other = lax.ppermute(own, AXES, partners())
    spot = jnp.stack([lax.axis_index("wa"), lax.rem(lax.axis_index("pb"), 2)])
    shape = (4, 4, 4, 24, 128)
    sums = main(
        kmap.reshape(16), spot, own.reshape(shape), other.reshape(shape), screened[0]
    )
    sums = jnp.sum(exchange(sums, planes()), axis=0)
    sums = sums.reshape(8, 2, 64).transpose(1, 0, 2).reshape(16, 64)
    sums = jnp.sum(exchange(sums, lines()), axis=0)
    return sums.reshape(2, 2, 16)[:, :, :12].reshape(2, 24)


def solution(mesh):
    in_specs = (
        P("wa", None, "pb"),
        P("wa", None, "pb"),
        P("wa", "pb"),
        P("pb", "wa", None),
        P("pb", None),
    )
    return jax.shard_map(
        shards, mesh=mesh, in_specs=in_specs, out_specs=P("wa", "pb"), check_vma=False
    )
```

```python
import itertools

import jax
import jax.numpy as jnp
from jax import lax
from jax.experimental import pallas as pl
from jax.experimental.pallas import tpu as pltpu
from jax.sharding import PartitionSpec as P

AXES = ("pb", "wa")
NX, NY, NZ, NC = 4, 4, 16, 2
F32 = jnp.float32
BF16 = jnp.bfloat16
NT = (((1,), (1,)), ((), ()))


def place(x, y, z, c):
    return (((z % 8) * NX + x) * NC + c) * 8 + y * 2 + z // 8


def lines():
    spans = itertools.product(range(NX), range(NY), range(NC))
    return [[place(x, y, z, c) for z in range(NZ)] for x, y, c in spans]


def planes():
    spots = list(itertools.product(range(NY), range(NX), range(NC)))
    return [[place(x, y, z, c) for y, x, c in spots] for z in range(NZ)]


def sheets():
    spots = list(itertools.product(range(NY), range(NX)))
    spans = itertools.product(range(NZ), range(NC))
    return [[place(x, y, z, c) for y, x in spots] for z, c in spans]


def partners():
    return [(i, i ^ 8) for i in range(NX * NY * NZ * NC)]


def exchange(x, groups):
    return lax.all_to_all(x, AXES, 0, 0, tiled=True, axis_index_groups=groups)


def line_kernel(val_in, cond_in, trial_in, out_ref, val_ref, cond_ref, trial_ref, wide, sems):
    pairs = ((val_in, val_ref), (cond_in, cond_ref), (trial_in, trial_ref))
    copies = [
        pltpu.make_async_copy(there, here, sems.at[i])
        for i, (there, here) in enumerate(pairs)
    ]
    for copy in copies:
        copy.start()
    wide[...] = jnp.zeros_like(wide)
    for copy in copies:
        copy.wait()
    for k in range(2):
        base = k * 24
        for band in range(12):
            wide[base + band : base + band + 1, 0:16] = cond_ref[
                band, k : k + 1, :
            ].astype(F32)
        for half in range(2):
            wide[base + 12 + half : base + 13 + half, 0:12] = trial_ref[
                k : k + 1, half * 12 : half * 12 + 12
            ].astype(F32)
        wide[base + 16 : base + 24, 0:16] = val_ref[k].astype(F32)
    line = wide[pl.ds(0, 6, stride=8), :]
    for slot in range(1, 8):
        line += pltpu.roll(wide[pl.ds(slot, 6, stride=8), :], slot * 16, 1)
    block = jnp.concatenate([line, jnp.zeros((2, 128), F32)], axis=0).astype(BF16)
    for dest in range(out_ref.shape[0]):
        out_ref[dest] = block


def lined(val, cond, trial):
    there = pl.BlockSpec(memory_space=pltpu.HBM)
    return pl.pallas_call(
        line_kernel,
        out_shape=jax.ShapeDtypeStruct((NZ, 8, 128), BF16),
        in_specs=[there, there, there],
        out_specs=pl.BlockSpec(memory_space=pltpu.VMEM),
        scratch_shapes=[
            pltpu.VMEM(val.shape, BF16),
            pltpu.VMEM(cond.shape, BF16),
            pltpu.VMEM(trial.shape, BF16),
            pltpu.VMEM((48, 128), F32),
            pltpu.SemaphoreType.DMA((3,)),
        ],
        name="line",
    )(val, cond, trial)


def swap_kernel(in_ref, out_ref, wide):
    wide[...] = in_ref[...].astype(F32).reshape(128, 128)
    row = lax.broadcasted_iota(jnp.int32, (8, 128), 0)
    lane = lax.broadcasted_iota(jnp.int32, (8, 128), 1) // 16
    turn = lax.rem(row - lane + 8, 8)
    tiles = []
    for zh in range(2):
        for a in range(6):
            tile = wide[pl.ds(zh * 64 + a, 8, stride=8), :]
            done = jnp.where(turn == 0, tile, 0.0)
            for step in range(1, 8):
                moved = pltpu.roll(pltpu.roll(tile, step, 0), 128 - 16 * step, 1)
                done = jnp.where(turn == step, moved, done)
            tiles.append(done)
    block = jnp.concatenate(tiles, axis=0).astype(BF16)
    for dest in range(out_ref.shape[0]):
        out_ref[dest] = block


def swap(x):
    vmem = pl.BlockSpec(memory_space=pltpu.VMEM)
    return pl.pallas_call(
        swap_kernel,
        out_shape=jax.ShapeDtypeStruct((NX * NY, 96, 128), BF16),
        in_specs=[vmem],
        out_specs=vmem,
        scratch_shapes=[pltpu.VMEM((128, 128), F32)],
        compiler_params=pltpu.CompilerParams(vmem_limit_bytes=4 << 20),
        name="swap",
    )(x)


def main_kernel(
    table_ref, own_ref, other_ref, w_ref, o_ref,
    wt, psi, loc, t1, t2, mixed, wa, wb, acc, back,
):
    spot, core = table_ref[16], table_ref[17]
    lane16 = lax.broadcasted_iota(jnp.int32, (8, 128), 1) // 16
    own_row = lane16 == lax.broadcasted_iota(jnp.int32, (8, 128), 0)
    lane24 = lax.broadcasted_iota(jnp.int32, (24, 128), 1) // 16

    sides = (own_ref, other_ref)

    def seat(xc):
        return xc - xc % 2 + (core if xc % 2 == 0 else 1 - core)

    for z in range(8):
        turned = w_ref[:, z * 128 : (z + 1) * 128].astype(F32).T.astype(BF16)
        for xc in range(8):
            rows = pl.ds(pl.multiple_of(seat(xc) * 128 + z * 16, 16), 16)
            wt[rows, :] = turned[xc * 16 : (xc + 1) * 16]

    def bands(k, rows):
        y, k4 = k // 4, lax.rem(k, 4)
        return jnp.concatenate(
            [sides[n % 2][y, n // 2, k4, rows, :] for n in range(8)], axis=1
        )

    def spread_one(k, j):
        y, k4 = k // 4, lax.rem(k, 4)
        local = jnp.zeros((24, 128), F32)
        for x in range(4):
            for near in range(2):
                xc = x * 2 + (core if near == 0 else 1 - core)
                tile = sides[near][y, x, k4].astype(F32)
                psi[k, x * 2 + near] = tile
                shift = lax.rem((xc - spot + 8) * 16, 128)
                local = jnp.where(lane24 == xc, pltpu.roll(tile, shift, 1), local)
        loc[k] = local

    def weigh_one(k, j):
        local = loc[k]
        rows = []
        for u in range(8):
            for xh in range(2):
                xc = xh * 4 + u // 2
                at = psi[k, seat(xc), pl.ds(12 + u % 2, 8, stride=0), :]
                rows.append(jnp.where(own_row, at, 0.0))
        left = jnp.concatenate(rows, axis=0).astype(BF16)
        right = jnp.concatenate([local[0:16].astype(BF16)] * 8, axis=0)
        first = jnp.dot(left, right, preferred_element_type=F32).astype(BF16)
        for u in range(8):
            t1[k, :, u * 128 : (u + 1) * 128] = first[u * 16 : (u + 1) * 16]
        flat = jnp.concatenate(
            [psi[k, seat(xc), 12:14, :] for xc in range(8)], axis=0
        )
        val = local[16:24].astype(BF16)
        none = jnp.zeros_like(val)
        right = jnp.concatenate(
            [
                jnp.concatenate([val, none], axis=1),
                jnp.concatenate([none, val], axis=1),
            ],
            axis=0,
        )
        second = jnp.dot(flat.T.astype(BF16), right, preferred_element_type=F32)
        for xh in range(2):
            mixed[j, xh] = second[:, xh * 128 : (xh + 1) * 128]
        for d in range(12):
            both = [mixed[j, xh, pl.ds(d, 8, stride=16), :] for xh in range(2)]
            t2[k, :, d * 128 : (d + 1) * 128] = jnp.concatenate(both, axis=0).astype(BF16)

    def spread(i, carry):
        for j in range(4):
            spread_one(i * 4 + j, j)
        return carry

    lax.fori_loop(0, 4, spread, 0)

    upper = lax.broadcasted_iota(jnp.int32, (8, 128), 0) >= 4

    def same(at, row):
        return at[pl.ds(row, 8, stride=0), :]

    def grown(at, row):
        one = same(at, row)
        return jnp.concatenate([one, one], axis=0).astype(BF16)

    def pairs_of(k, j):
        p = table_ref[k]
        val_here = bands(k, slice(16, 24))
        val_here = jnp.concatenate([val_here, val_here], axis=0)
        low = bands(p, slice(0, 8))
        low = jnp.concatenate([low, low], axis=0)
        high = []
        for n in range(8):
            tile = psi[p, n, 8:16, :]
            tile = jnp.where(upper, pltpu.roll(tile, 4, 0), tile)
            high.append(jnp.concatenate([tile, tile], axis=0).astype(BF16))
        high = jnp.concatenate(high, axis=1)

        def twins(at, one, two):
            return jnp.concatenate(
                [
                    jnp.concatenate(
                        [same(psi.at[at, n], one), same(psi.at[at, n], two)], axis=0
                    ).astype(BF16)
                    for n in range(8)
                ],
                axis=1,
            )

        def fours(at, first):
            wide = []
            for n in range(8):
                rows = [same(psi.at[at, n], first + i) for i in range(4)]
                halves = [
                    jnp.where(upper, rows[i + 1], rows[i]) for i in range(0, 4, 2)
                ]
                wide.append(jnp.concatenate(halves, axis=0).astype(BF16))
            return jnp.concatenate(wide, axis=1)

        parts = [twins(p, 16 + u, 17 + u) * val_here for u in range(0, 8, 2)]
        parts += [twins(k, d, d + 1) * low for d in range(0, 12, 2)]
        parts += [fours(k, d) * high for d in range(0, 12, 4)]
        ww = jnp.dot(
            jnp.concatenate(parts, axis=0), wt[...], preferred_element_type=F32
        )
        wa[j] = ww[0:64]
        for d in range(12):
            tail = ww[160 + d // 2 * 8 : 168 + d // 2 * 8]
            if d % 2:
                tail = pltpu.roll(tail, 4, 0)
            wb[j, d * 16 : (d + 1) * 16] = jnp.concatenate(
                [ww[64 + d * 8 : 72 + d * 8], tail], axis=0
            ).astype(BF16)

    def close(k, j):
        p = table_ref[k]
        cond = loc[k, 0:16, :].astype(BF16)
        vals = [grown(loc.at[p], 16 + v) for v in range(8)]
        lf = jnp.concatenate(
            [
                jnp.concatenate(
                    [grown(wa.at[j], u * 8 + v) * cond for v in range(8)],
                    axis=0,
                )
                for u in range(8)
            ],
            axis=1,
        )
        lb = jnp.concatenate(
            [
                jnp.concatenate(
                    [wb[j, d * 16 : (d + 1) * 16] * vals[v] for v in range(8)], axis=0
                )
                for d in range(12)
            ],
            axis=1,
        )
        acc[k] = lax.dot_general(t1[p], lf, NT, preferred_element_type=F32)
        back[p] = lax.dot_general(t2[k], lb, NT, preferred_element_type=F32)

    for k in range(16):
        weigh_one(k, k % 8)
        if k == 7:
            pairs_of(0, 0)

    def pair(i, carry):
        k = i * 2
        pairs_of(k + 1, 1)
        close(k, 0)
        pairs_of(k + 2, 0)
        close(k + 1, 1)
        return carry

    lax.fori_loop(0, 7, pair, 0)
    pairs_of(15, 1)
    close(14, 0)
    close(15, 1)

    lane32 = lax.broadcasted_iota(jnp.int32, (8, 128), 1) // 32
    for y in range(4):
        for xh in range(2):
            rows = slice(xh * 8, (xh + 1) * 8)
            held = [acc[y * 4 + i, rows] + back[y * 4 + i, rows] for i in range(4)]
            for vv in range(4):
                done = held[vv]
                for k4 in range(4):
                    if k4 != vv:
                        moved = pltpu.roll(held[k4], (k4 - vv) * 32 % 128, 1)
                        done = jnp.where(lane32 == k4, moved, done)
                o_ref[y * 8 + xh * 4 + vv] = done


def main(table, own, other, weights):
    vmem = pl.BlockSpec(memory_space=pltpu.VMEM)
    smem = pl.BlockSpec(memory_space=pltpu.SMEM)
    return pl.pallas_call(
        main_kernel,
        out_shape=jax.ShapeDtypeStruct((32, 8, 128), F32),
        in_specs=[smem, vmem, vmem, vmem],
        out_specs=vmem,
        scratch_shapes=[
            pltpu.VMEM((1024, 128), BF16),
            pltpu.VMEM((16, 8, 24, 128), F32),
            pltpu.VMEM((16, 24, 128), F32),
            pltpu.VMEM((16, 16, 1024), BF16),
            pltpu.VMEM((16, 16, 1536), BF16),
            pltpu.VMEM((8, 2, 128, 128), F32),
            pltpu.VMEM((2, 64, 128), F32),
            pltpu.VMEM((2, 192, 128), BF16),
            pltpu.VMEM((16, 16, 128), F32),
            pltpu.VMEM((16, 16, 128), F32),
        ],
        compiler_params=pltpu.CompilerParams(vmem_limit_bytes=16 << 20),
        name="act",
    )(table, own, other, weights)


def shards(psi_val, psi_cond, trials, screened, kmap):
    along = exchange(lined(psi_val, psi_cond.transpose(1, 0, 2), trials), lines())
    own = exchange(swap(along), sheets())
    other = lax.ppermute(own, AXES, partners())
    spot = jnp.stack([lax.axis_index("wa"), lax.axis_index("pb") & 1])
    table = jnp.concatenate([kmap.reshape(16), spot])
    shape = (4, 4, 4, 24, 128)
    sums = main(
        table, own.reshape(shape), other.reshape(shape), screened[0]
    )
    sums = jnp.sum(exchange(sums, planes()), axis=0)
    sums = sums.reshape(8, 2, 64).transpose(1, 0, 2).reshape(16, 64)
    sums = jnp.sum(exchange(sums, lines()), axis=0)
    return sums.reshape(2, 2, 16)[:, :, :12].reshape(2, 24)


def solution(mesh):
    in_specs = (
        P("wa", None, "pb"),
        P("wa", None, "pb"),
        P("wa", "pb"),
        P("pb", "wa", None),
        P("pb", None),
    )
    return jax.shard_map(
        shards, mesh=mesh, in_specs=in_specs, out_specs=P("wa", "pb"), check_vma=False
    )
```

```python
import itertools

import jax
import jax.numpy as jnp
from jax import lax
from jax.experimental import pallas as pl
from jax.experimental.pallas import tpu as pltpu
from jax.sharding import PartitionSpec as P

AXES = ("pb", "wa")
NX, NY, NZ, NC = 4, 4, 16, 2
F32 = jnp.float32
BF16 = jnp.bfloat16
NT = (((1,), (1,)), ((), ()))


def place(x, y, z, c):
    return (((z % 8) * NX + x) * NC + c) * 8 + y * 2 + z // 8


def lines():
    spans = itertools.product(range(NX), range(NY), range(NC))
    return [[place(x, y, z, c) for z in range(NZ)] for x, y, c in spans]


def planes():
    spots = list(itertools.product(range(NY), range(NX), range(NC)))
    return [[place(x, y, z, c) for y, x, c in spots] for z in range(NZ)]


def sheets():
    spots = list(itertools.product(range(NY), range(NX)))
    spans = itertools.product(range(NZ), range(NC))
    return [[place(x, y, z, c) for y, x in spots] for z, c in spans]


def partners():
    return [(i, i ^ 8) for i in range(NX * NY * NZ * NC)]


def exchange(x, groups):
    return lax.all_to_all(x, AXES, 0, 0, tiled=True, axis_index_groups=groups)


def line_kernel(val_in, cond_in, trial_in, out_ref, val_ref, cond_ref, trial_ref, wide, sems):
    pairs = ((val_in, val_ref), (cond_in, cond_ref), (trial_in, trial_ref))
    copies = [
        pltpu.make_async_copy(there, here, sems.at[i])
        for i, (there, here) in enumerate(pairs)
    ]
    for copy in copies:
        copy.start()
    wide[...] = jnp.zeros_like(wide)
    for copy in copies:
        copy.wait()
    for k in range(2):
        base = k * 24
        for band in range(12):
            wide[base + band : base + band + 1, 0:16] = cond_ref[
                band, k : k + 1, :
            ].astype(F32)
        for half in range(2):
            wide[base + 12 + half : base + 13 + half, 0:12] = trial_ref[
                k : k + 1, half * 12 : half * 12 + 12
            ].astype(F32)
        wide[base + 16 : base + 24, 0:16] = val_ref[k].astype(F32)
    line = wide[pl.ds(0, 6, stride=8), :]
    for slot in range(1, 8):
        line += pltpu.roll(wide[pl.ds(slot, 6, stride=8), :], slot * 16, 1)
    block = jnp.concatenate([line, jnp.zeros((2, 128), F32)], axis=0).astype(BF16)
    for dest in range(out_ref.shape[0]):
        out_ref[dest] = block


def lined(val, cond, trial):
    there = pl.BlockSpec(memory_space=pltpu.HBM)
    return pl.pallas_call(
        line_kernel,
        out_shape=jax.ShapeDtypeStruct((NZ, 8, 128), BF16),
        in_specs=[there, there, there],
        out_specs=pl.BlockSpec(memory_space=pltpu.VMEM),
        scratch_shapes=[
            pltpu.VMEM(val.shape, BF16),
            pltpu.VMEM(cond.shape, BF16),
            pltpu.VMEM(trial.shape, BF16),
            pltpu.VMEM((48, 128), F32),
            pltpu.SemaphoreType.DMA((3,)),
        ],
        name="line",
    )(val, cond, trial)


def swap_kernel(in_ref, out_ref, wide):
    wide[...] = in_ref[...].astype(F32).reshape(128, 128)
    row = lax.broadcasted_iota(jnp.int32, (8, 128), 0)
    lane = lax.broadcasted_iota(jnp.int32, (8, 128), 1) // 16
    turn = lax.rem(row - lane + 8, 8)
    tiles = []
    for zh in range(2):
        for a in range(6):
            tile = wide[pl.ds(zh * 64 + a, 8, stride=8), :]
            done = jnp.where(turn == 0, tile, 0.0)
            for step in range(1, 8):
                moved = pltpu.roll(pltpu.roll(tile, step, 0), 128 - 16 * step, 1)
                done = jnp.where(turn == step, moved, done)
            tiles.append(done)
    block = jnp.concatenate(tiles, axis=0).astype(BF16)
    for dest in range(out_ref.shape[0]):
        out_ref[dest] = block


def swap(x):
    vmem = pl.BlockSpec(memory_space=pltpu.VMEM)
    return pl.pallas_call(
        swap_kernel,
        out_shape=jax.ShapeDtypeStruct((NX * NY, 96, 128), BF16),
        in_specs=[vmem],
        out_specs=vmem,
        scratch_shapes=[pltpu.VMEM((128, 128), F32)],
        compiler_params=pltpu.CompilerParams(vmem_limit_bytes=4 << 20),
        name="swap",
    )(x)


def main_kernel(
    table_ref, own_ref, other_ref, w_ref, o_ref,
    wt, psi, loc, t1, t2, mixed, wa, wb, acc, back,
):
    spot, core = table_ref[16], table_ref[17]
    lane16 = lax.broadcasted_iota(jnp.int32, (8, 128), 1) // 16
    own_row = lane16 == lax.broadcasted_iota(jnp.int32, (8, 128), 0)
    lane24 = lax.broadcasted_iota(jnp.int32, (24, 128), 1) // 16

    sides = (own_ref, other_ref)

    def seat(xc):
        return xc - xc % 2 + (core if xc % 2 == 0 else 1 - core)

    for z in range(8):
        turned = w_ref[:, z * 128 : (z + 1) * 128].astype(F32).T.astype(BF16)
        for xc in range(8):
            rows = pl.ds(pl.multiple_of(seat(xc) * 128 + z * 16, 16), 16)
            wt[rows, :] = turned[xc * 16 : (xc + 1) * 16]

    def bands(k, rows):
        y, k4 = divmod(k, 4) if isinstance(k, int) else (k // 4, lax.rem(k, 4))
        return jnp.concatenate(
            [sides[n % 2][y, n // 2, k4, rows, :] for n in range(8)], axis=1
        )

    def spread_one(k, j):
        y, k4 = divmod(k, 4) if isinstance(k, int) else (k // 4, lax.rem(k, 4))
        local = jnp.zeros((24, 128), F32)
        for x in range(4):
            for near in range(2):
                xc = x * 2 + (core if near == 0 else 1 - core)
                tile = sides[near][y, x, k4].astype(F32)
                psi[k, x * 2 + near] = tile
                shift = lax.rem((xc - spot + 8) * 16, 128)
                local = jnp.where(lane24 == xc, pltpu.roll(tile, shift, 1), local)
        loc[k] = local

    def weigh_one(k, j):
        local = loc[k]
        rows = []
        for xh in range(2):
            for u in range(8):
                xc = xh * 4 + u // 2
                at = psi[k, seat(xc), pl.ds(12 + u % 2, 8, stride=0), :]
                rows.append(jnp.where(own_row, at, 0.0))
        left = jnp.concatenate(rows, axis=0).astype(BF16)
        right = jnp.concatenate([local[0:16].astype(BF16)] * 8, axis=0)
        first = jnp.dot(left, right, preferred_element_type=F32)
        for xh in range(2):
            t1[k, xh] = first[xh * 64 : (xh + 1) * 64]
        flat = jnp.concatenate(
            [psi[k, seat(xc), 12:14, :] for xc in range(8)], axis=0
        )
        val = local[16:24].astype(BF16)
        none = jnp.zeros_like(val)
        right = jnp.concatenate(
            [
                jnp.concatenate([val, none], axis=1),
                jnp.concatenate([none, val], axis=1),
            ],
            axis=0,
        )
        second = jnp.dot(flat.T.astype(BF16), right, preferred_element_type=F32)
        for xh in range(2):
            mixed[j, xh] = second[:, xh * 128 : (xh + 1) * 128]
        for d in range(12):
            both = [mixed[j, xh, pl.ds(d, 8, stride=16), :] for xh in range(2)]
            t2[k, :, d * 128 : (d + 1) * 128] = jnp.concatenate(both, axis=0).astype(BF16)

    def spread(i, carry):
        for j in range(4):
            spread_one(i * 4 + j, j)
        return carry

    for i in range(4):
        spread(i, 0)

    upper = lax.broadcasted_iota(jnp.int32, (8, 128), 0) >= 4

    def same(at, row):
        return at[pl.ds(row, 8, stride=0), :]

    def grown(at, row):
        one = same(at, row)
        return jnp.concatenate([one, one], axis=0).astype(BF16)

    def pairs_of(k, j):
        p = table_ref[k]
        val_here = bands(k, slice(16, 24))
        val_here = jnp.concatenate([val_here, val_here], axis=0)
        low = bands(p, slice(0, 8))
        low = jnp.concatenate([low, low], axis=0)
        high = []
        for n in range(8):
            tile = psi[p, n, 8:16, :]
            tile = jnp.where(upper, pltpu.roll(tile, 4, 0), tile)
            high.append(jnp.concatenate([tile, tile], axis=0).astype(BF16))
        high = jnp.concatenate(high, axis=1)

        def twins(at, one, two):
            return jnp.concatenate(
                [
                    jnp.concatenate(
                        [same(psi.at[at, n], one), same(psi.at[at, n], two)], axis=0
                    ).astype(BF16)
                    for n in range(8)
                ],
                axis=1,
            )

        def fours(at, first):
            wide = []
            for n in range(8):
                rows = [same(psi.at[at, n], first + i) for i in range(4)]
                halves = [
                    jnp.where(upper, rows[i + 1], rows[i]) for i in range(0, 4, 2)
                ]
                wide.append(jnp.concatenate(halves, axis=0).astype(BF16))
            return jnp.concatenate(wide, axis=1)

        def some(i):
            if i == 0:
                return [twins(p, 16 + u, 17 + u) * val_here for u in range(0, 8, 2)]
            if i == 1:
                return [twins(k, d, d + 1) * low for d in range(0, 6, 2)] + [
                    fours(k, 0) * high
                ]
            return [twins(k, d, d + 1) * low for d in range(6, 12, 2)] + [
                fours(k, d) * high for d in (4, 8)
            ]

        def dot(i):
            return jnp.dot(
                jnp.concatenate(some(i), axis=0), wt[...], preferred_element_type=F32
            )

        def finish(got):
            wa[j] = got[0]
            for d in range(12):
                piece = got[1] if d < 6 else got[2]
                first = piece[d % 6 * 8 : d % 6 * 8 + 8]
                if d < 4:
                    tail = got[1][48 + d // 2 * 8 : 56 + d // 2 * 8]
                else:
                    tail = got[2][48 + (d - 4) // 2 * 8 : 56 + (d - 4) // 2 * 8]
                if d % 2:
                    tail = pltpu.roll(tail, 4, 0)
                wb[j, d * 16 : (d + 1) * 16] = jnp.concatenate(
                    [first, tail], axis=0
                ).astype(BF16)

        return some, finish

    def pairs_two(k0, j0, k1, j1):
        some0, finish0 = pairs_of(k0, j0)
        some1, finish1 = pairs_of(k1, j1)
        for some, finish in ((some0, finish0), (some1, finish1)):
            got = jnp.dot(
                jnp.concatenate(some(0) + some(1) + some(2), axis=0),
                wt[...],
                preferred_element_type=F32,
            )
            finish([got[0:64], got[64:128], got[128:208]])

    def close(k, j):
        p = table_ref[k]
        cond = loc[k, 0:16, :].astype(BF16)
        vals = [grown(loc.at[p], 16 + v) for v in range(8)]
        lb = jnp.concatenate(
            [
                jnp.concatenate(
                    [wb[j, d * 16 : (d + 1) * 16] * vals[v] for v in range(8)], axis=0
                )
                for d in range(12)
            ],
            axis=1,
        )
        tiles = []
        for xh in range(2):
            for v in range(8):
                total = same(wa.at[j], v) * t1[p, xh, 0:8, :]
                for u in range(1, 8):
                    total += same(wa.at[j], u * 8 + v) * t1[p, xh, u * 8 : u * 8 + 8, :]
                tiles.append(total)
        left = jnp.concatenate(tiles, axis=0).astype(BF16)
        right = jnp.concatenate([cond, jnp.zeros((112, 128), BF16)], axis=0)
        out = lax.dot_general(left, right, NT, preferred_element_type=F32)
        for xh in range(2):
            total = out[xh * 64 : xh * 64 + 8]
            for v in range(1, 8):
                at = xh * 64 + v * 8
                total += pltpu.roll(out[at : at + 8], v * 16, 1)
            acc[k, xh * 8 : (xh + 1) * 8, :] = total
        back[p] = lax.dot_general(t2[k], lb, NT, preferred_element_type=F32)

    for k in range(16):
        weigh_one(k, k % 8)
        if k == 7:
            pairs_two(0, 0, 1, 1)

    def pair(i, carry):
        k = i * 4
        for n in range(4):
            at, slot = k + 2 + n, (2 + n) % 4
            some, finish = pairs_of(at, slot)
            got = jnp.dot(
                jnp.concatenate(some(0) + some(1) + some(2), axis=0),
                wt[...],
                preferred_element_type=F32,
            )
            finish([got[0:64], got[64:128], got[128:208]])
            close(k + n, n)
        return carry

    for i in range(3):
        pair(i, 0)
    pairs_two(14, 2, 15, 3)
    close(12, 0)
    close(13, 1)
    close(14, 2)
    close(15, 3)

    lane32 = lax.broadcasted_iota(jnp.int32, (8, 128), 1) // 32
    for y in range(4):
        for xh in range(2):
            rows = slice(xh * 8, (xh + 1) * 8)
            held = [acc[y * 4 + i, rows] + back[y * 4 + i, rows] for i in range(4)]
            for vv in range(4):
                done = held[vv]
                for k4 in range(4):
                    if k4 != vv:
                        moved = pltpu.roll(held[k4], (k4 - vv) * 32 % 128, 1)
                        done = jnp.where(lane32 == k4, moved, done)
                o_ref[y * 8 + xh * 4 + vv] = done


def main(table, own, other, weights):
    vmem = pl.BlockSpec(memory_space=pltpu.VMEM)
    smem = pl.BlockSpec(memory_space=pltpu.SMEM)
    return pl.pallas_call(
        main_kernel,
        out_shape=jax.ShapeDtypeStruct((32, 8, 128), F32),
        in_specs=[smem, vmem, vmem, vmem],
        out_specs=vmem,
        scratch_shapes=[
            pltpu.VMEM((1024, 128), BF16),
            pltpu.VMEM((16, 8, 24, 128), F32),
            pltpu.VMEM((16, 24, 128), F32),
            pltpu.VMEM((16, 2, 64, 128), F32),
            pltpu.VMEM((16, 16, 1536), BF16),
            pltpu.VMEM((8, 2, 128, 128), F32),
            pltpu.VMEM((4, 64, 128), F32),
            pltpu.VMEM((4, 192, 128), BF16),
            pltpu.VMEM((16, 16, 128), F32),
            pltpu.VMEM((16, 16, 128), F32),
        ],
        compiler_params=pltpu.CompilerParams(vmem_limit_bytes=16 << 20),
        name="act",
    )(table, own, other, weights)


def shards(psi_val, psi_cond, trials, screened, kmap):
    along = exchange(lined(psi_val, psi_cond.transpose(1, 0, 2), trials), lines())
    own = exchange(swap(along), sheets())
    other = lax.ppermute(own, AXES, partners())
    spot = jnp.stack([lax.axis_index("wa"), lax.axis_index("pb") & 1])
    table = jnp.concatenate([kmap.reshape(16), spot])
    shape = (4, 4, 4, 24, 128)
    sums = main(
        table, own.reshape(shape), other.reshape(shape), screened[0]
    )
    sums = jnp.sum(exchange(sums, planes()), axis=0)
    sums = sums.reshape(8, 2, 64).transpose(1, 0, 2).reshape(16, 64)
    sums = jnp.sum(exchange(sums, lines()), axis=0)
    return sums.reshape(2, 2, 16)[:, :, :12].reshape(2, 24)


def solution(mesh):
    in_specs = (
        P("wa", None, "pb"),
        P("wa", None, "pb"),
        P("wa", "pb"),
        P("pb", "wa", None),
        P("pb", None),
    )
    return jax.shard_map(
        shards, mesh=mesh, in_specs=in_specs, out_specs=P("wa", "pb"), check_vma=False
    )
```

```python
import itertools

import jax
import jax.numpy as jnp
from jax import lax
from jax.experimental import pallas as pl
from jax.experimental.pallas import tpu as pltpu
from jax.sharding import PartitionSpec as P

AXES = ("pb", "wa")
NX, NY, NZ, NC = 4, 4, 16, 2
F32 = jnp.float32
BF16 = jnp.bfloat16
NT = (((1,), (1,)), ((), ()))


def place(x, y, z, c):
    return (((z % 8) * NX + x) * NC + c) * 8 + y * 2 + z // 8


def lines():
    spans = itertools.product(range(NX), range(NY), range(NC))
    return [[place(x, y, z, c) for z in range(NZ)] for x, y, c in spans]


def planes():
    spots = list(itertools.product(range(NY), range(NX), range(NC)))
    return [[place(x, y, z, c) for y, x, c in spots] for z in range(NZ)]


def sheets():
    spots = list(itertools.product(range(NY), range(NX)))
    spans = itertools.product(range(NZ), range(NC))
    return [[place(x, y, z, c) for y, x in spots] for z, c in spans]


def partners():
    return [(i, i ^ 8) for i in range(NX * NY * NZ * NC)]


def exchange(x, groups):
    return lax.all_to_all(x, AXES, 0, 0, tiled=True, axis_index_groups=groups)


def line_kernel(val_in, cond_in, trial_in, out_ref, val_ref, cond_ref, trial_ref, wide, sems):
    pairs = ((val_in, val_ref), (cond_in, cond_ref), (trial_in, trial_ref))
    copies = [
        pltpu.make_async_copy(there, here, sems.at[i])
        for i, (there, here) in enumerate(pairs)
    ]
    for copy in copies:
        copy.start()
    wide[...] = jnp.zeros_like(wide)
    for copy in copies:
        copy.wait()
    for k in range(2):
        base = k * 24
        for band in range(12):
            wide[base + band : base + band + 1, 0:16] = cond_ref[
                band, k : k + 1, :
            ].astype(F32)
        for half in range(2):
            wide[base + 12 + half : base + 13 + half, 0:12] = trial_ref[
                k : k + 1, half * 12 : half * 12 + 12
            ].astype(F32)
        wide[base + 16 : base + 24, 0:16] = val_ref[k].astype(F32)
    line = wide[pl.ds(0, 6, stride=8), :]
    for slot in range(1, 8):
        line += pltpu.roll(wide[pl.ds(slot, 6, stride=8), :], slot * 16, 1)
    block = jnp.concatenate([line, jnp.zeros((2, 128), F32)], axis=0).astype(BF16)
    for dest in range(out_ref.shape[0]):
        out_ref[dest] = block


def lined(val, cond, trial):
    there = pl.BlockSpec(memory_space=pltpu.HBM)
    return pl.pallas_call(
        line_kernel,
        out_shape=jax.ShapeDtypeStruct((NZ, 8, 128), BF16),
        in_specs=[there, there, there],
        out_specs=pl.BlockSpec(memory_space=pltpu.VMEM),
        scratch_shapes=[
            pltpu.VMEM(val.shape, BF16),
            pltpu.VMEM(cond.shape, BF16),
            pltpu.VMEM(trial.shape, BF16),
            pltpu.VMEM((48, 128), F32),
            pltpu.SemaphoreType.DMA((3,)),
        ],
        compiler_params=pltpu.CompilerParams(vmem_limit_bytes=4 << 20),
        name="line",
    )(*(pltpu.with_memory_space_constraint(a, pltpu.HBM) for a in (val, cond, trial)))


def swap_kernel(in_ref, out_ref, wide):
    wide[...] = in_ref[...].astype(F32).reshape(128, 128)
    row = lax.broadcasted_iota(jnp.int32, (8, 128), 0)
    lane = lax.broadcasted_iota(jnp.int32, (8, 128), 1) // 16
    turn = lax.rem(row - lane + 8, 8)
    tiles = []
    for zh in range(2):
        for a in range(6):
            tile = wide[pl.ds(zh * 64 + a, 8, stride=8), :]
            done = jnp.where(turn == 0, tile, 0.0)
            for step in range(1, 8):
                moved = pltpu.roll(pltpu.roll(tile, step, 0), 128 - 16 * step, 1)
                done = jnp.where(turn == step, moved, done)
            tiles.append(done)
    block = jnp.concatenate(tiles, axis=0).astype(BF16)
    for dest in range(out_ref.shape[0]):
        out_ref[dest] = block


def swap(x):
    vmem = pl.BlockSpec(memory_space=pltpu.VMEM)
    return pl.pallas_call(
        swap_kernel,
        out_shape=jax.ShapeDtypeStruct((NX * NY, 96, 128), BF16),
        in_specs=[vmem],
        out_specs=vmem,
        scratch_shapes=[pltpu.VMEM((128, 128), F32)],
        compiler_params=pltpu.CompilerParams(vmem_limit_bytes=4 << 20),
        name="swap",
    )(x)


def main_kernel(
    table_ref, own_ref, other_ref, w_ref, o_ref,
    wt, psi, loc, t1, t2, mixed, wa, wb, acc, back,
):
    spot, core = table_ref[16], table_ref[17]
    lane16 = lax.broadcasted_iota(jnp.int32, (8, 128), 1) // 16
    own_row = lane16 == lax.broadcasted_iota(jnp.int32, (8, 128), 0)
    lane24 = lax.broadcasted_iota(jnp.int32, (24, 128), 1) // 16

    sides = (own_ref, other_ref)

    def seat(xc):
        return xc - xc % 2 + (core if xc % 2 == 0 else 1 - core)

    for z in range(8):
        turned = w_ref[:, z * 128 : (z + 1) * 128].astype(F32).T.astype(BF16)
        for xc in range(8):
            rows = pl.ds(pl.multiple_of(seat(xc) * 128 + z * 16, 16), 16)
            wt[rows, :] = turned[xc * 16 : (xc + 1) * 16]

    def bands(k, rows):
        y, k4 = divmod(k, 4) if isinstance(k, int) else (k // 4, lax.rem(k, 4))
        return jnp.concatenate(
            [sides[n % 2][y, n // 2, k4, rows, :] for n in range(8)], axis=1
        )

    def spread_one(k, j):
        y, k4 = divmod(k, 4) if isinstance(k, int) else (k // 4, lax.rem(k, 4))
        local = jnp.zeros((24, 128), F32)
        for x in range(4):
            for near in range(2):
                xc = x * 2 + (core if near == 0 else 1 - core)
                tile = sides[near][y, x, k4].astype(F32)
                psi[k, x * 2 + near] = tile
                shift = lax.rem((xc - spot + 8) * 16, 128)
                local = jnp.where(lane24 == xc, pltpu.roll(tile, shift, 1), local)
        loc[k] = local

    def weigh_one(k, j):
        local = loc[k]
        rows = []
        for xh in range(2):
            for u in range(8):
                xc = xh * 4 + u // 2
                at = psi[k, seat(xc), pl.ds(12 + u % 2, 8, stride=0), :]
                rows.append(jnp.where(own_row, at, 0.0))
        left = jnp.concatenate(rows, axis=0).astype(BF16)
        right = jnp.concatenate([local[0:16].astype(BF16)] * 8, axis=0)
        first = jnp.dot(left, right, preferred_element_type=F32)
        for xh in range(2):
            t1[k, xh] = first[xh * 64 : (xh + 1) * 64]
        flat = jnp.concatenate(
            [psi[k, seat(xc), 12:14, :] for xc in range(8)], axis=0
        )
        val = local[16:24].astype(BF16)
        none = jnp.zeros_like(val)
        right = jnp.concatenate(
            [
                jnp.concatenate([val, none], axis=1),
                jnp.concatenate([none, val], axis=1),
            ],
            axis=0,
        )
        second = jnp.dot(flat.T.astype(BF16), right, preferred_element_type=F32)
        for xh in range(2):
            mixed[j, xh] = second[:, xh * 128 : (xh + 1) * 128]
        for d in range(12):
            both = [mixed[j, xh, pl.ds(d, 8, stride=16), :] for xh in range(2)]
            t2[k, :, d * 128 : (d + 1) * 128] = jnp.concatenate(both, axis=0).astype(BF16)

    def spread(i, carry):
        for j in range(4):
            spread_one(i * 4 + j, j)
        return carry

    for i in range(4):
        spread(i, 0)

    upper = lax.broadcasted_iota(jnp.int32, (8, 128), 0) >= 4

    def same(at, row):
        return at[pl.ds(row, 8, stride=0), :]

    def grown(at, row):
        one = same(at, row)
        return jnp.concatenate([one, one], axis=0).astype(BF16)

    def pairs_of(k, j):
        p = table_ref[k]
        val_here = bands(k, slice(16, 24))
        val_here = jnp.concatenate([val_here, val_here], axis=0)
        low = bands(p, slice(0, 8))
        low = jnp.concatenate([low, low], axis=0)
        high = []
        for n in range(8):
            tile = psi[p, n, 8:16, :]
            tile = jnp.where(upper, pltpu.roll(tile, 4, 0), tile)
            high.append(jnp.concatenate([tile, tile], axis=0).astype(BF16))
        high = jnp.concatenate(high, axis=1)

        def twins(at, one, two):
            return jnp.concatenate(
                [
                    jnp.concatenate(
                        [same(psi.at[at, n], one), same(psi.at[at, n], two)], axis=0
                    ).astype(BF16)
                    for n in range(8)
                ],
                axis=1,
            )

        def fours(at, first):
            wide = []
            for n in range(8):
                rows = [same(psi.at[at, n], first + i) for i in range(4)]
                halves = [
                    jnp.where(upper, rows[i + 1], rows[i]) for i in range(0, 4, 2)
                ]
                wide.append(jnp.concatenate(halves, axis=0).astype(BF16))
            return jnp.concatenate(wide, axis=1)

        def some(i):
            if i == 0:
                return [twins(p, 16 + u, 17 + u) * val_here for u in range(0, 8, 2)]
            if i == 1:
                return [twins(k, d, d + 1) * low for d in range(0, 6, 2)] + [
                    fours(k, 0) * high
                ]
            return [twins(k, d, d + 1) * low for d in range(6, 12, 2)] + [
                fours(k, d) * high for d in (4, 8)
            ]

        def dot(i):
            return jnp.dot(
                jnp.concatenate(some(i), axis=0), wt[...], preferred_element_type=F32
            )

        def finish(got):
            wa[j] = got[0]
            for d in range(12):
                piece = got[1] if d < 6 else got[2]
                first = piece[d % 6 * 8 : d % 6 * 8 + 8]
                if d < 4:
                    tail = got[1][48 + d // 2 * 8 : 56 + d // 2 * 8]
                else:
                    tail = got[2][48 + (d - 4) // 2 * 8 : 56 + (d - 4) // 2 * 8]
                if d % 2:
                    tail = pltpu.roll(tail, 4, 0)
                wb[j, d * 16 : (d + 1) * 16] = jnp.concatenate(
                    [first, tail], axis=0
                ).astype(BF16)

        return some, finish

    def pairs_two(k0, j0, k1, j1):
        some0, finish0 = pairs_of(k0, j0)
        some1, finish1 = pairs_of(k1, j1)
        for some, finish in ((some0, finish0), (some1, finish1)):
            got = jnp.dot(
                jnp.concatenate(some(0) + some(1) + some(2), axis=0),
                wt[...],
                preferred_element_type=F32,
            )
            finish([got[0:64], got[64:128], got[128:208]])

    def close(k, j):
        p = table_ref[k]
        cond = loc[k, 0:16, :].astype(BF16)
        vals = [grown(loc.at[p], 16 + v) for v in range(8)]
        lb = jnp.concatenate(
            [
                jnp.concatenate(
                    [wb[j, d * 16 : (d + 1) * 16] * vals[v] for v in range(8)], axis=0
                )
                for d in range(12)
            ],
            axis=1,
        )
        tiles = []
        for xh in range(2):
            for v in range(8):
                total = same(wa.at[j], v) * t1[p, xh, 0:8, :]
                for u in range(1, 8):
                    total += same(wa.at[j], u * 8 + v) * t1[p, xh, u * 8 : u * 8 + 8, :]
                tiles.append(total)
        left = jnp.concatenate(tiles, axis=0).astype(BF16)
        right = jnp.concatenate([cond, jnp.zeros((112, 128), BF16)], axis=0)
        out = lax.dot_general(left, right, NT, preferred_element_type=F32)
        for xh in range(2):
            total = out[xh * 64 : xh * 64 + 8]
            for v in range(1, 8):
                at = xh * 64 + v * 8
                total += pltpu.roll(out[at : at + 8], v * 16, 1)
            acc[k, xh * 8 : (xh + 1) * 8, :] = total
        back[p] = lax.dot_general(t2[k], lb, NT, preferred_element_type=F32)

    for k in range(16):
        weigh_one(k, k % 8)
        if k == 7:
            pairs_two(0, 0, 1, 1)

    def pair(i, carry):
        k = i * 4
        for n in range(4):
            at, slot = k + 2 + n, (2 + n) % 4
            some, finish = pairs_of(at, slot)
            got = jnp.dot(
                jnp.concatenate(some(0) + some(1) + some(2), axis=0),
                wt[...],
                preferred_element_type=F32,
            )
            finish([got[0:64], got[64:128], got[128:208]])
            close(k + n, n)
        return carry

    for i in range(3):
        pair(i, 0)
    pairs_two(14, 2, 15, 3)
    close(12, 0)
    close(13, 1)
    close(14, 2)
    close(15, 3)

    lane32 = lax.broadcasted_iota(jnp.int32, (8, 128), 1) // 32
    for y in range(4):
        for xh in range(2):
            rows = slice(xh * 8, (xh + 1) * 8)
            held = [acc[y * 4 + i, rows] + back[y * 4 + i, rows] for i in range(4)]
            for vv in range(4):
                done = held[vv]
                for k4 in range(4):
                    if k4 != vv:
                        moved = pltpu.roll(held[k4], (k4 - vv) * 32 % 128, 1)
                        done = jnp.where(lane32 == k4, moved, done)
                o_ref[y * 8 + xh * 4 + vv] = done


def main(table, own, other, weights):
    vmem = pl.BlockSpec(memory_space=pltpu.VMEM)
    smem = pl.BlockSpec(memory_space=pltpu.SMEM)
    return pl.pallas_call(
        main_kernel,
        out_shape=jax.ShapeDtypeStruct((32, 8, 128), F32),
        in_specs=[smem, vmem, vmem, vmem],
        out_specs=vmem,
        scratch_shapes=[
            pltpu.VMEM((1024, 128), BF16),
            pltpu.VMEM((16, 8, 24, 128), F32),
            pltpu.VMEM((16, 24, 128), F32),
            pltpu.VMEM((16, 2, 64, 128), F32),
            pltpu.VMEM((16, 16, 1536), BF16),
            pltpu.VMEM((8, 2, 128, 128), F32),
            pltpu.VMEM((4, 64, 128), F32),
            pltpu.VMEM((4, 192, 128), BF16),
            pltpu.VMEM((16, 16, 128), F32),
            pltpu.VMEM((16, 16, 128), F32),
        ],
        compiler_params=pltpu.CompilerParams(vmem_limit_bytes=16 << 20),
        name="act",
    )(table, own, other, weights)


def shards(psi_val, psi_cond, trials, screened, kmap):
    along = exchange(lined(psi_val, psi_cond.transpose(1, 0, 2), trials), lines())
    own = exchange(swap(along), sheets())
    other = lax.ppermute(own, AXES, partners())
    spot = jnp.stack([lax.axis_index("wa"), lax.axis_index("pb") & 1])
    table = jnp.concatenate([kmap.reshape(16), spot])
    shape = (4, 4, 4, 24, 128)
    sums = main(
        table, own.reshape(shape), other.reshape(shape), screened[0]
    )
    sums = jnp.sum(exchange(sums, planes()), axis=0)
    sums = sums.reshape(8, 2, 64).transpose(1, 0, 2).reshape(16, 64)
    sums = jnp.sum(exchange(sums, lines()), axis=0)
    return sums.reshape(2, 2, 16)[:, :, :12].reshape(2, 24)


def solution(mesh):
    in_specs = (
        P("wa", None, "pb"),
        P("wa", None, "pb"),
        P("wa", "pb"),
        P("pb", "wa", None),
        P("pb", None),
    )
    return jax.shard_map(
        shards, mesh=mesh, in_specs=in_specs, out_specs=P("wa", "pb"), check_vma=False
    )
```

```python
import itertools

import jax
import jax.numpy as jnp
from jax import lax
from jax.experimental import pallas as pl
from jax.experimental.pallas import tpu as pltpu
from jax.sharding import PartitionSpec as P

AXES = ("pb", "wa")
NX, NY, NZ, NC = 4, 4, 16, 2
F32 = jnp.float32
BF16 = jnp.bfloat16
NT = (((1,), (1,)), ((), ()))


def place(x, y, z, c):
    return (((z % 8) * NX + x) * NC + c) * 8 + y * 2 + z // 8


def lines():
    spans = itertools.product(range(NX), range(NY), range(NC))
    return [[place(x, y, z, c) for z in range(NZ)] for x, y, c in spans]


def planes():
    spots = list(itertools.product(range(NY), range(NX), range(NC)))
    return [[place(x, y, z, c) for y, x, c in spots] for z in range(NZ)]


def sheets():
    spots = list(itertools.product(range(NY), range(NX)))
    spans = itertools.product(range(NZ), range(NC))
    return [[place(x, y, z, c) for y, x in spots] for z, c in spans]


def partners():
    return [(i, i ^ 8) for i in range(NX * NY * NZ * NC)]


def exchange(x, groups):
    return lax.all_to_all(x, AXES, 0, 0, tiled=True, axis_index_groups=groups)


def line_kernel(val_in, cond_in, trial_in, out_ref, val_ref, cond_ref, trial_ref, wide, sems):
    pairs = ((val_in, val_ref), (cond_in, cond_ref), (trial_in, trial_ref))
    copies = [
        pltpu.make_async_copy(there, here, sems.at[i])
        for i, (there, here) in enumerate(pairs)
    ]
    for copy in copies:
        copy.start()
    wide[...] = jnp.zeros_like(wide)
    for copy in copies:
        copy.wait()
    for k in range(2):
        base = k * 24
        for band in range(12):
            wide[base + band : base + band + 1, 0:16] = cond_ref[
                band, k : k + 1, :
            ].astype(F32)
        for half in range(2):
            wide[base + 12 + half : base + 13 + half, 0:12] = trial_ref[
                k : k + 1, half * 12 : half * 12 + 12
            ].astype(F32)
        wide[base + 16 : base + 24, 0:16] = val_ref[k].astype(F32)
    line = wide[pl.ds(0, 6, stride=8), :]
    for slot in range(1, 8):
        line += pltpu.roll(wide[pl.ds(slot, 6, stride=8), :], slot * 16, 1)
    block = jnp.concatenate([line, jnp.zeros((2, 128), F32)], axis=0).astype(BF16)
    for dest in range(out_ref.shape[0]):
        out_ref[dest] = block


def lined(val, cond, trial):
    there = pl.BlockSpec(memory_space=pltpu.HBM)
    return pl.pallas_call(
        line_kernel,
        out_shape=jax.ShapeDtypeStruct((NZ, 8, 128), BF16),
        in_specs=[there, there, there],
        out_specs=pl.BlockSpec(memory_space=pltpu.VMEM),
        scratch_shapes=[
            pltpu.VMEM(val.shape, BF16),
            pltpu.VMEM(cond.shape, BF16),
            pltpu.VMEM(trial.shape, BF16),
            pltpu.VMEM((48, 128), F32),
            pltpu.SemaphoreType.DMA((3,)),
        ],
        compiler_params=pltpu.CompilerParams(vmem_limit_bytes=4 << 20),
        name="line",
    )(*(pltpu.with_memory_space_constraint(a, pltpu.HBM) for a in (val, cond, trial)))


def swap_kernel(in_ref, out_ref, wide):
    wide[...] = in_ref[...].astype(F32).reshape(128, 128)
    row = lax.broadcasted_iota(jnp.int32, (8, 128), 0)
    lane = lax.broadcasted_iota(jnp.int32, (8, 128), 1) // 16
    turn = lax.rem(row - lane + 8, 8)
    tiles = []
    for zh in range(2):
        for a in range(6):
            tile = wide[pl.ds(zh * 64 + a, 8, stride=8), :]
            done = jnp.where(turn == 0, tile, 0.0)
            for step in range(1, 8):
                moved = pltpu.roll(pltpu.roll(tile, step, 0), 128 - 16 * step, 1)
                done = jnp.where(turn == step, moved, done)
            tiles.append(done)
    block = jnp.concatenate(tiles, axis=0).astype(BF16)
    for dest in range(out_ref.shape[0]):
        out_ref[dest] = block


def swap(x):
    vmem = pl.BlockSpec(memory_space=pltpu.VMEM)
    return pl.pallas_call(
        swap_kernel,
        out_shape=jax.ShapeDtypeStruct((NX * NY, 96, 128), BF16),
        in_specs=[vmem],
        out_specs=vmem,
        scratch_shapes=[pltpu.VMEM((128, 128), F32)],
        compiler_params=pltpu.CompilerParams(vmem_limit_bytes=4 << 20),
        name="swap",
    )(x)


def turn_kernel(table_ref, w_ref, out_ref):
    core = table_ref[17]
    for z in range(8):
        turned = w_ref[:, z * 128 : (z + 1) * 128].astype(F32).T.astype(BF16)
        for xc in range(8):
            seat = xc - xc % 2 + (core if xc % 2 == 0 else 1 - core)
            rows = pl.ds(pl.multiple_of(seat * 128 + z * 16, 16), 16)
            out_ref[rows, :] = turned[xc * 16 : (xc + 1) * 16]


def turn(table, weights):
    vmem = pl.BlockSpec(memory_space=pltpu.VMEM)
    return pl.pallas_call(
        turn_kernel,
        out_shape=jax.ShapeDtypeStruct((1024, 128), BF16),
        in_specs=[pl.BlockSpec(memory_space=pltpu.SMEM), vmem],
        out_specs=vmem,
        compiler_params=pltpu.CompilerParams(vmem_limit_bytes=4 << 20),
        cost_estimate=pl.CostEstimate(
            flops=1 << 20, bytes_accessed=1 << 19, transcendentals=0
        ),
        name="turn",
    )(table, weights)


def main_kernel(
    table_ref, own_ref, other_ref, wt, o_ref,
    psi, loc, t1, t2, mixed, wa, wb, acc, back,
):
    spot, core = table_ref[16], table_ref[17]
    lane16 = lax.broadcasted_iota(jnp.int32, (8, 128), 1) // 16
    own_row = lane16 == lax.broadcasted_iota(jnp.int32, (8, 128), 0)
    lane24 = lax.broadcasted_iota(jnp.int32, (24, 128), 1) // 16

    sides = (own_ref, other_ref)

    def seat(xc):
        return xc - xc % 2 + (core if xc % 2 == 0 else 1 - core)

    def bands(k, rows):
        y, k4 = divmod(k, 4) if isinstance(k, int) else (k // 4, lax.rem(k, 4))
        return jnp.concatenate(
            [sides[n % 2][y, n // 2, k4, rows, :] for n in range(8)], axis=1
        )

    def spread_one(k, j):
        y, k4 = divmod(k, 4) if isinstance(k, int) else (k // 4, lax.rem(k, 4))
        local = jnp.zeros((24, 128), F32)
        for x in range(4):
            for near in range(2):
                xc = x * 2 + (core if near == 0 else 1 - core)
                tile = sides[near][y, x, k4].astype(F32)
                psi[k, x * 2 + near] = tile
                shift = lax.rem((xc - spot + 8) * 16, 128)
                local = jnp.where(lane24 == xc, pltpu.roll(tile, shift, 1), local)
        loc[k] = local

    def weigh_one(k, j):
        local = loc[k]
        rows = []
        for xh in range(2):
            for u in range(8):
                xc = xh * 4 + u // 2
                at = psi[k, seat(xc), pl.ds(12 + u % 2, 8, stride=0), :]
                rows.append(jnp.where(own_row, at, 0.0))
        left = jnp.concatenate(rows, axis=0).astype(BF16)
        right = jnp.concatenate([local[0:16].astype(BF16)] * 8, axis=0)
        first = jnp.dot(left, right, preferred_element_type=F32)
        for xh in range(2):
            t1[k, xh] = first[xh * 64 : (xh + 1) * 64]
        flat = jnp.concatenate(
            [psi[k, seat(xc), 12:14, :] for xc in range(8)], axis=0
        )
        val = local[16:24].astype(BF16)
        none = jnp.zeros_like(val)
        right = jnp.concatenate(
            [
                jnp.concatenate([val, none], axis=1),
                jnp.concatenate([none, val], axis=1),
            ],
            axis=0,
        )
        second = jnp.dot(flat.T.astype(BF16), right, preferred_element_type=F32)
        for xh in range(2):
            mixed[k, xh] = second[:, xh * 128 : (xh + 1) * 128]
        for d in range(6):
            both = [mixed[k, xh, pl.ds(d, 8, stride=16), :] for xh in range(2)]
            t2[k, :, d * 128 : (d + 1) * 128] = jnp.concatenate(both, axis=0).astype(BF16)

    def spread(i, carry):
        for j in range(4):
            spread_one(i * 4 + j, j)
        return carry

    for i in range(4):
        spread(i, 0)

    upper = lax.broadcasted_iota(jnp.int32, (8, 128), 0) >= 4

    def same(at, row):
        return at[pl.ds(row, 8, stride=0), :]

    def grown(at, row):
        one = same(at, row)
        return jnp.concatenate([one, one], axis=0).astype(BF16)

    def pairs_of(k, j):
        p = table_ref[k]
        val_here = bands(k, slice(16, 24))
        val_here = jnp.concatenate([val_here, val_here], axis=0)
        low = bands(p, slice(0, 8))
        low = jnp.concatenate([low, low], axis=0)
        high = []
        for n in range(8):
            tile = psi[p, n, 8:16, :]
            tile = jnp.where(upper, pltpu.roll(tile, 4, 0), tile)
            high.append(jnp.concatenate([tile, tile], axis=0).astype(BF16))
        high = jnp.concatenate(high, axis=1)

        def twins(at, one, two):
            return jnp.concatenate(
                [
                    jnp.concatenate(
                        [same(psi.at[at, n], one), same(psi.at[at, n], two)], axis=0
                    ).astype(BF16)
                    for n in range(8)
                ],
                axis=1,
            )

        def fours(at, first):
            wide = []
            for n in range(8):
                rows = [same(psi.at[at, n], first + i) for i in range(4)]
                halves = [
                    jnp.where(upper, rows[i + 1], rows[i]) for i in range(0, 4, 2)
                ]
                wide.append(jnp.concatenate(halves, axis=0).astype(BF16))
            return jnp.concatenate(wide, axis=1)

        def some(i):
            if i == 0:
                return [twins(p, 16 + u, 17 + u) * val_here for u in range(0, 8, 2)]
            if i == 1:
                return [twins(k, d, d + 1) * low for d in range(0, 6, 2)] + [
                    fours(k, 0) * high
                ]
            return [twins(k, d, d + 1) * low for d in range(6, 12, 2)] + [
                fours(k, d) * high for d in (4, 8)
            ]

        def dot(i):
            return jnp.dot(
                jnp.concatenate(some(i), axis=0), wt[...], preferred_element_type=F32
            )

        def finish(got):
            wa[j] = got[0]
            for d in range(12):
                piece = got[1] if d < 6 else got[2]
                first = piece[d % 6 * 8 : d % 6 * 8 + 8]
                if d < 4:
                    tail = got[1][48 + d // 2 * 8 : 56 + d // 2 * 8]
                else:
                    tail = got[2][48 + (d - 4) // 2 * 8 : 56 + (d - 4) // 2 * 8]
                if d % 2:
                    tail = pltpu.roll(tail, 4, 0)
                wb[j, d * 16 : (d + 1) * 16] = jnp.concatenate([first, tail], axis=0)

        return some, finish

    def pairs_two(k0, j0, k1, j1):
        some0, finish0 = pairs_of(k0, j0)
        some1, finish1 = pairs_of(k1, j1)
        for some, finish in ((some0, finish0), (some1, finish1)):
            got = jnp.dot(
                jnp.concatenate(some(0) + some(1) + some(2), axis=0),
                wt[...],
                preferred_element_type=F32,
            )
            finish([got[0:64], got[64:128], got[128:208]])

    def close(k, j):
        p = table_ref[k]
        cond = loc[k, 0:16, :].astype(BF16)
        vals = [grown(loc.at[p], 16 + v) for v in range(8)]
        lb = []
        for d in range(6):
            row = wb[j, d * 16 : (d + 1) * 16].astype(BF16)
            lb.append(jnp.concatenate([row * vals[v] for v in range(8)], axis=0))
        lb = jnp.concatenate(lb, axis=1)
        tiles = []
        for xh in range(2):
            for v in range(8):
                total = same(wa.at[j], v) * t1[p, xh, 0:8, :]
                for u in range(1, 8):
                    total += same(wa.at[j], u * 8 + v) * t1[p, xh, u * 8 : u * 8 + 8, :]
                tiles.append(total)
        left = jnp.concatenate(tiles, axis=0).astype(BF16)
        right = jnp.concatenate([cond, jnp.zeros((112, 128), BF16)], axis=0)
        out = lax.dot_general(left, right, NT, preferred_element_type=F32)
        for xh in range(2):
            total = out[xh * 64 : xh * 64 + 8]
            for v in range(1, 8):
                at = xh * 64 + v * 8
                total += pltpu.roll(out[at : at + 8], v * 16, 1)
            acc[k, xh * 8 : (xh + 1) * 8, :] = total
        part = lax.dot_general(t2[k], lb, NT, preferred_element_type=F32)
        cols = [
            [mixed[k, xh, pl.ds(d, 8, stride=16), :] for d in range(6, 12)]
            for xh in range(2)
        ]
        tiles = []
        for c in range(12):
            rows = [same(wb.at[j], d * 16 + c) for d in range(6, 12)]
            for xh in range(2):
                total = rows[0] * cols[xh][0]
                for one, two in zip(rows[1:], cols[xh][1:]):
                    total += one * two
                tiles.append(total)
        left = jnp.concatenate(tiles, axis=0).astype(BF16)
        val = loc[p, 16:24, :]
        none = jnp.zeros((15, 128), F32)
        right = [val[v : v + 1] if i == 0 else none for v in range(8) for i in range(2)]
        right = jnp.concatenate(right, axis=0).astype(BF16)
        out = lax.dot_general(left, right, NT, preferred_element_type=F32)
        for xh in range(2):
            total = part[xh * 8 : xh * 8 + 8] + out[xh * 8 : xh * 8 + 8]
            for c in range(1, 12):
                at = c * 16 + xh * 8
                total += pltpu.roll(out[at : at + 8], c, 1)
            back[p, xh * 8 : (xh + 1) * 8, :] = total

    for k in range(16):
        weigh_one(k, k % 8)
        if k == 7:
            pairs_two(0, 0, 1, 1)

    def pair(i, carry):
        k = i * 4
        for n in range(4):
            at, slot = k + 2 + n, (2 + n) % 4
            some, finish = pairs_of(at, slot)
            got = jnp.dot(
                jnp.concatenate(some(0) + some(1) + some(2), axis=0),
                wt[...],
                preferred_element_type=F32,
            )
            finish([got[0:64], got[64:128], got[128:208]])
            close(k + n, n)
        return carry

    for i in range(3):
        pair(i, 0)
    pairs_two(14, 2, 15, 3)
    close(12, 0)
    close(13, 1)
    close(14, 2)
    close(15, 3)

    lane32 = lax.broadcasted_iota(jnp.int32, (8, 128), 1) // 32
    for y in range(4):
        for xh in range(2):
            rows = slice(xh * 8, (xh + 1) * 8)
            held = [acc[y * 4 + i, rows] + back[y * 4 + i, rows] for i in range(4)]
            for vv in range(4):
                done = held[vv]
                for k4 in range(4):
                    if k4 != vv:
                        moved = pltpu.roll(held[k4], (k4 - vv) * 32 % 128, 1)
                        done = jnp.where(lane32 == k4, moved, done)
                o_ref[y * 8 + xh * 4 + vv] = done


def main(table, own, other, weights):
    vmem = pl.BlockSpec(memory_space=pltpu.VMEM)
    smem = pl.BlockSpec(memory_space=pltpu.SMEM)
    return pl.pallas_call(
        main_kernel,
        out_shape=jax.ShapeDtypeStruct((32, 8, 128), F32),
        in_specs=[smem, vmem, vmem, vmem],
        out_specs=vmem,
        scratch_shapes=[
            pltpu.VMEM((16, 8, 24, 128), F32),
            pltpu.VMEM((16, 24, 128), F32),
            pltpu.VMEM((16, 2, 64, 128), F32),
            pltpu.VMEM((16, 16, 768), BF16),
            pltpu.VMEM((16, 2, 128, 128), F32),
            pltpu.VMEM((4, 64, 128), F32),
            pltpu.VMEM((4, 192, 128), F32),
            pltpu.VMEM((16, 16, 128), F32),
            pltpu.VMEM((16, 16, 128), F32),
        ],
        compiler_params=pltpu.CompilerParams(vmem_limit_bytes=16 << 20),
        name="act",
    )(table, own, other, weights)


def shards(psi_val, psi_cond, trials, screened, kmap):
    along = exchange(lined(psi_val, psi_cond.transpose(1, 0, 2), trials), lines())
    own = exchange(swap(along), sheets())
    other = lax.ppermute(own, AXES, partners())
    spot = jnp.stack([lax.axis_index("wa"), lax.axis_index("pb") & 1])
    table = jnp.concatenate([kmap.reshape(16), spot])
    shape = (4, 4, 4, 24, 128)
    sums = main(
        table, own.reshape(shape), other.reshape(shape), turn(table, screened[0])
    )
    sums = jnp.sum(exchange(sums, planes()), axis=0)
    sums = sums.reshape(8, 2, 64).transpose(1, 0, 2).reshape(16, 64)
    sums = jnp.sum(exchange(sums, lines()), axis=0)
    return sums.reshape(2, 2, 16)[:, :, :12].reshape(2, 24)


def solution(mesh):
    in_specs = (
        P("wa", None, "pb"),
        P("wa", None, "pb"),
        P("wa", "pb"),
        P("pb", "wa", None),
        P("pb", None),
    )
    return jax.shard_map(
        shards, mesh=mesh, in_specs=in_specs, out_specs=P("wa", "pb"), check_vma=False
    )
```

```python
import itertools

import jax
import jax.numpy as jnp
from jax import lax
from jax.experimental import pallas as pl
from jax.experimental.pallas import tpu as pltpu
from jax.sharding import PartitionSpec as P

AXES = ("pb", "wa")
NX, NY, NZ, NC = 4, 4, 16, 2
F32 = jnp.float32
BF16 = jnp.bfloat16
NT = (((1,), (1,)), ((), ()))


def place(x, y, z, c):
    return (((z % 8) * NX + x) * NC + c) * 8 + y * 2 + z // 8


def lines():
    spans = itertools.product(range(NX), range(NY), range(NC))
    return [[place(x, y, z, c) for z in range(NZ)] for x, y, c in spans]


def planes():
    spots = list(itertools.product(range(NX), range(NY), range(NC)))
    return [[place(x, y, z, c) for x, y, c in spots] for z in range(NZ)]


def sheets():
    spots = list(itertools.product(range(NY), range(NX)))
    spans = itertools.product(range(NZ), range(NC))
    return [[place(x, y, z, c) for y, x in spots] for z, c in spans]


def partners():
    return [(i, i ^ 8) for i in range(NX * NY * NZ * NC)]


def exchange(x, groups):
    return lax.all_to_all(x, AXES, 0, 0, tiled=True, axis_index_groups=groups)


def line_kernel(val_in, cond_in, trial_in, out_ref, val_ref, cond_ref, trial_ref, wide, sems):
    pairs = ((val_in, val_ref), (cond_in, cond_ref), (trial_in, trial_ref))
    copies = [
        pltpu.make_async_copy(there, here, sems.at[i])
        for i, (there, here) in enumerate(pairs)
    ]
    for copy in copies:
        copy.start()
    wide[...] = jnp.zeros_like(wide)
    for copy in copies:
        copy.wait()
    for k in range(2):
        base = k * 24
        for band in range(12):
            wide[base + band : base + band + 1, 0:16] = cond_ref[
                band, k : k + 1, :
            ].astype(F32)
        for half in range(2):
            wide[base + 12 + half : base + 13 + half, 0:12] = trial_ref[
                k : k + 1, half * 12 : half * 12 + 12
            ].astype(F32)
        wide[base + 16 : base + 24, 0:16] = val_ref[k].astype(F32)
    line = wide[pl.ds(0, 6, stride=8), :]
    for slot in range(1, 8):
        line += pltpu.roll(wide[pl.ds(slot, 6, stride=8), :], slot * 16, 1)
    block = jnp.concatenate([line, jnp.zeros((2, 128), F32)], axis=0).astype(BF16)
    for dest in range(out_ref.shape[0]):
        out_ref[dest] = block


def lined(val, cond, trial):
    there = pl.BlockSpec(memory_space=pltpu.HBM)
    return pl.pallas_call(
        line_kernel,
        out_shape=jax.ShapeDtypeStruct((NZ, 8, 128), BF16),
        in_specs=[there, there, there],
        out_specs=pl.BlockSpec(memory_space=pltpu.VMEM),
        scratch_shapes=[
            pltpu.VMEM(val.shape, BF16),
            pltpu.VMEM(cond.shape, BF16),
            pltpu.VMEM(trial.shape, BF16),
            pltpu.VMEM((48, 128), F32),
            pltpu.SemaphoreType.DMA((3,)),
        ],
        compiler_params=pltpu.CompilerParams(vmem_limit_bytes=4 << 20),
        name="line",
    )(*(pltpu.with_memory_space_constraint(a, pltpu.HBM) for a in (val, cond, trial)))


def swap_kernel(in_ref, out_ref, wide):
    wide[...] = in_ref[...].astype(F32).reshape(128, 128)
    row = lax.broadcasted_iota(jnp.int32, (8, 128), 0)
    lane = lax.broadcasted_iota(jnp.int32, (8, 128), 1) // 16
    turn = lax.rem(row - lane + 8, 8)
    tiles = []
    for zh in range(2):
        for a in range(6):
            tile = wide[pl.ds(zh * 64 + a, 8, stride=8), :]
            done = jnp.where(turn == 0, tile, 0.0)
            for step in range(1, 8):
                moved = pltpu.roll(pltpu.roll(tile, step, 0), 128 - 16 * step, 1)
                done = jnp.where(turn == step, moved, done)
            tiles.append(done)
    block = jnp.concatenate(tiles, axis=0).astype(BF16)
    for dest in range(out_ref.shape[0]):
        out_ref[dest] = block


def swap(x):
    vmem = pl.BlockSpec(memory_space=pltpu.VMEM)
    return pl.pallas_call(
        swap_kernel,
        out_shape=jax.ShapeDtypeStruct((NX * NY, 96, 128), BF16),
        in_specs=[vmem],
        out_specs=vmem,
        scratch_shapes=[pltpu.VMEM((128, 128), F32)],
        compiler_params=pltpu.CompilerParams(vmem_limit_bytes=4 << 20),
        name="swap",
    )(x)


def turn_kernel(table_ref, w_ref, out_ref):
    core = table_ref[17]
    for z in range(8):
        turned = w_ref[:, z * 128 : (z + 1) * 128].astype(F32).T.astype(BF16)
        for xc in range(8):
            seat = xc - xc % 2 + (core if xc % 2 == 0 else 1 - core)
            rows = pl.ds(pl.multiple_of(seat * 128 + z * 16, 16), 16)
            out_ref[rows, :] = turned[xc * 16 : (xc + 1) * 16]


def turn(table, weights):
    vmem = pl.BlockSpec(memory_space=pltpu.VMEM)
    return pl.pallas_call(
        turn_kernel,
        out_shape=jax.ShapeDtypeStruct((1024, 128), BF16),
        in_specs=[pl.BlockSpec(memory_space=pltpu.SMEM), vmem],
        out_specs=vmem,
        compiler_params=pltpu.CompilerParams(vmem_limit_bytes=4 << 20),
        cost_estimate=pl.CostEstimate(
            flops=1 << 20, bytes_accessed=1 << 19, transcendentals=0
        ),
        name="turn",
    )(table, weights)


def main_kernel(
    table_ref, own_ref, other_ref, wt, o_ref,
    psi, loc, t1, t2, mixed, wa, wb, acc, back,
):
    spot, core = table_ref[16], table_ref[17]
    lane16 = lax.broadcasted_iota(jnp.int32, (8, 128), 1) // 16
    own_row = lane16 == lax.broadcasted_iota(jnp.int32, (8, 128), 0)
    lane24 = lax.broadcasted_iota(jnp.int32, (24, 128), 1) // 16

    sides = (own_ref, other_ref)

    def seat(xc):
        return xc - xc % 2 + (core if xc % 2 == 0 else 1 - core)

    def bands(k, rows):
        y, k4 = divmod(k, 4) if isinstance(k, int) else (k // 4, lax.rem(k, 4))
        return jnp.concatenate(
            [sides[n % 2][y, n // 2, k4, rows, :] for n in range(8)], axis=1
        )

    def spread_one(k, j):
        y, k4 = divmod(k, 4) if isinstance(k, int) else (k // 4, lax.rem(k, 4))
        local = jnp.zeros((24, 128), F32)
        for x in range(4):
            for near in range(2):
                xc = x * 2 + (core if near == 0 else 1 - core)
                tile = sides[near][y, x, k4].astype(F32)
                psi[k, x * 2 + near] = tile
                shift = lax.rem((xc - spot + 8) * 16, 128)
                local = jnp.where(lane24 == xc, pltpu.roll(tile, shift, 1), local)
        loc[k] = local

    def weigh_one(k, j):
        local = loc[k]
        rows = []
        for xh in range(2):
            for u in range(8):
                xc = xh * 4 + u // 2
                at = psi[k, seat(xc), pl.ds(12 + u % 2, 8, stride=0), :]
                rows.append(jnp.where(own_row, at, 0.0))
        left = jnp.concatenate(rows, axis=0).astype(BF16)
        right = jnp.concatenate([local[0:16].astype(BF16)] * 8, axis=0)
        first = jnp.dot(left, right, preferred_element_type=F32)
        for xh in range(2):
            t1[k, xh] = first[xh * 64 : (xh + 1) * 64]
        flat = jnp.concatenate(
            [psi[k, seat(xc), 12:14, :] for xc in range(8)], axis=0
        )
        val = local[16:24].astype(BF16)
        none = jnp.zeros_like(val)
        right = jnp.concatenate(
            [
                jnp.concatenate([val, none], axis=1),
                jnp.concatenate([none, val], axis=1),
            ],
            axis=0,
        )
        second = jnp.dot(flat.T.astype(BF16), right, preferred_element_type=F32)
        for xh in range(2):
            mixed[k, xh] = second[:, xh * 128 : (xh + 1) * 128]
        for d in range(6):
            both = [mixed[k, xh, pl.ds(d, 8, stride=16), :] for xh in range(2)]
            t2[k, :, d * 128 : (d + 1) * 128] = jnp.concatenate(both, axis=0).astype(BF16)

    def spread(i, carry):
        for j in range(4):
            spread_one(i * 4 + j, j)
        return carry

    for i in range(4):
        spread(i, 0)

    upper = lax.broadcasted_iota(jnp.int32, (8, 128), 0) >= 4

    def same(at, row):
        return at[pl.ds(row, 8, stride=0), :]

    def grown(at, row):
        one = same(at, row)
        return jnp.concatenate([one, one], axis=0).astype(BF16)

    def pairs_of(k, j):
        p = table_ref[k]
        val_here = bands(k, slice(16, 24))
        val_here = jnp.concatenate([val_here, val_here], axis=0)
        low = bands(p, slice(0, 8))
        low = jnp.concatenate([low, low], axis=0)
        high = []
        for n in range(8):
            tile = psi[p, n, 8:16, :]
            tile = jnp.where(upper, pltpu.roll(tile, 4, 0), tile)
            high.append(jnp.concatenate([tile, tile], axis=0).astype(BF16))
        high = jnp.concatenate(high, axis=1)

        def twins(at, one, two):
            return jnp.concatenate(
                [
                    jnp.concatenate(
                        [same(psi.at[at, n], one), same(psi.at[at, n], two)], axis=0
                    ).astype(BF16)
                    for n in range(8)
                ],
                axis=1,
            )

        def fours(at, first):
            wide = []
            for n in range(8):
                rows = [same(psi.at[at, n], first + i) for i in range(4)]
                halves = [
                    jnp.where(upper, rows[i + 1], rows[i]) for i in range(0, 4, 2)
                ]
                wide.append(jnp.concatenate(halves, axis=0).astype(BF16))
            return jnp.concatenate(wide, axis=1)

        def some(i):
            if i == 0:
                return [twins(p, 16 + u, 17 + u) * val_here for u in range(0, 8, 2)]
            if i == 1:
                return [twins(k, d, d + 1) * low for d in range(0, 6, 2)] + [
                    fours(k, 0) * high
                ]
            return [twins(k, d, d + 1) * low for d in range(6, 12, 2)] + [
                fours(k, d) * high for d in (4, 8)
            ]

        def dot(i):
            return jnp.dot(
                jnp.concatenate(some(i), axis=0), wt[...], preferred_element_type=F32
            )

        def finish(got):
            wa[j] = got[0]
            for d in range(12):
                piece = got[1] if d < 6 else got[2]
                first = piece[d % 6 * 8 : d % 6 * 8 + 8]
                if d < 4:
                    tail = got[1][48 + d // 2 * 8 : 56 + d // 2 * 8]
                else:
                    tail = got[2][48 + (d - 4) // 2 * 8 : 56 + (d - 4) // 2 * 8]
                if d % 2:
                    tail = pltpu.roll(tail, 4, 0)
                wb[j, d * 16 : (d + 1) * 16] = jnp.concatenate([first, tail], axis=0)

        return some, finish

    def pairs_two(k0, j0, k1, j1):
        some0, finish0 = pairs_of(k0, j0)
        some1, finish1 = pairs_of(k1, j1)
        for some, finish in ((some0, finish0), (some1, finish1)):
            got = jnp.dot(
                jnp.concatenate(some(0) + some(1) + some(2), axis=0),
                wt[...],
                preferred_element_type=F32,
            )
            finish([got[0:64], got[64:128], got[128:208]])

    def close(k, j):
        p = table_ref[k]
        cond = loc[k, 0:16, :].astype(BF16)
        vals = [grown(loc.at[p], 16 + v) for v in range(8)]
        lb = []
        for d in range(6):
            row = wb[j, d * 16 : (d + 1) * 16].astype(BF16)
            lb.append(jnp.concatenate([row * vals[v] for v in range(8)], axis=0))
        lb = jnp.concatenate(lb, axis=1)
        tiles = []
        for xh in range(2):
            for v in range(8):
                total = same(wa.at[j], v) * t1[p, xh, 0:8, :]
                for u in range(1, 8):
                    total += same(wa.at[j], u * 8 + v) * t1[p, xh, u * 8 : u * 8 + 8, :]
                tiles.append(total)
        left = jnp.concatenate(tiles, axis=0).astype(BF16)
        right = jnp.concatenate([cond, jnp.zeros((112, 128), BF16)], axis=0)
        out = lax.dot_general(left, right, NT, preferred_element_type=F32)
        for xh in range(2):
            total = out[xh * 64 : xh * 64 + 8]
            for v in range(1, 8):
                at = xh * 64 + v * 8
                total += pltpu.roll(out[at : at + 8], v * 16, 1)
            acc[k, xh * 8 : (xh + 1) * 8, :] = total
        part = lax.dot_general(t2[k], lb, NT, preferred_element_type=F32)
        cols = [
            [mixed[k, xh, pl.ds(d, 8, stride=16), :] for d in range(6, 12)]
            for xh in range(2)
        ]
        tiles = []
        for c in range(12):
            rows = [same(wb.at[j], d * 16 + c) for d in range(6, 12)]
            for xh in range(2):
                total = rows[0] * cols[xh][0]
                for one, two in zip(rows[1:], cols[xh][1:]):
                    total += one * two
                tiles.append(total)
        left = jnp.concatenate(tiles, axis=0).astype(BF16)
        val = loc[p, 16:24, :]
        none = jnp.zeros((15, 128), F32)
        right = [val[v : v + 1] if i == 0 else none for v in range(8) for i in range(2)]
        right = jnp.concatenate(right, axis=0).astype(BF16)
        out = lax.dot_general(left, right, NT, preferred_element_type=F32)
        for xh in range(2):
            total = part[xh * 8 : xh * 8 + 8] + out[xh * 8 : xh * 8 + 8]
            for c in range(1, 12):
                at = c * 16 + xh * 8
                total += pltpu.roll(out[at : at + 8], c, 1)
            back[p, xh * 8 : (xh + 1) * 8, :] = total

    for k in range(16):
        weigh_one(k, k % 8)
        if k == 7:
            pairs_two(0, 0, 1, 1)

    def pair(i, carry):
        k = i * 4
        for n in range(4):
            at, slot = k + 2 + n, (2 + n) % 4
            some, finish = pairs_of(at, slot)
            got = jnp.dot(
                jnp.concatenate(some(0) + some(1) + some(2), axis=0),
                wt[...],
                preferred_element_type=F32,
            )
            finish([got[0:64], got[64:128], got[128:208]])
            close(k + n, n)
        return carry

    for i in range(3):
        pair(i, 0)
    pairs_two(14, 2, 15, 3)
    close(12, 0)
    close(13, 1)
    close(14, 2)
    close(15, 3)

    lane32 = lax.broadcasted_iota(jnp.int32, (8, 128), 1) // 32
    for y in range(4):
        for xh in range(2):
            rows = slice(xh * 8, (xh + 1) * 8)
            held = [acc[y * 4 + i, rows] + back[y * 4 + i, rows] for i in range(4)]
            for vv in range(4):
                done = held[vv]
                for k4 in range(4):
                    if k4 != vv:
                        moved = pltpu.roll(held[k4], (k4 - vv) * 32 % 128, 1)
                        done = jnp.where(lane32 == k4, moved, done)
                o_ref[(xh * 2 + vv // 2) * 8 + y * 2 + vv % 2] = done


def main(table, own, other, weights):
    vmem = pl.BlockSpec(memory_space=pltpu.VMEM)
    smem = pl.BlockSpec(memory_space=pltpu.SMEM)
    return pl.pallas_call(
        main_kernel,
        out_shape=jax.ShapeDtypeStruct((32, 8, 128), F32),
        in_specs=[smem, vmem, vmem, vmem],
        out_specs=vmem,
        scratch_shapes=[
            pltpu.VMEM((16, 8, 24, 128), F32),
            pltpu.VMEM((16, 24, 128), F32),
            pltpu.VMEM((16, 2, 64, 128), F32),
            pltpu.VMEM((16, 16, 768), BF16),
            pltpu.VMEM((16, 2, 128, 128), F32),
            pltpu.VMEM((4, 64, 128), F32),
            pltpu.VMEM((4, 192, 128), F32),
            pltpu.VMEM((16, 16, 128), F32),
            pltpu.VMEM((16, 16, 128), F32),
        ],
        compiler_params=pltpu.CompilerParams(vmem_limit_bytes=16 << 20),
        name="act",
    )(table, own, other, weights)


def shards(psi_val, psi_cond, trials, screened, kmap):
    along = exchange(lined(psi_val, psi_cond.transpose(1, 0, 2), trials), lines())
    own = exchange(swap(along), sheets())
    other = lax.ppermute(own, AXES, partners())
    spot = jnp.stack([lax.axis_index("wa"), lax.axis_index("pb") & 1])
    table = jnp.concatenate([kmap.reshape(16), spot])
    shape = (4, 4, 4, 24, 128)
    sums = main(
        table, own.reshape(shape), other.reshape(shape), turn(table, screened[0])
    )
    sums = jnp.sum(exchange(sums, planes()), axis=0)
    sums = sums.reshape(8, 2, 64).transpose(1, 0, 2).reshape(16, 64)
    sums = jnp.sum(exchange(sums, lines()), axis=0)
    return sums.reshape(2, 2, 16)[:, :, :12].reshape(2, 24)


def solution(mesh):
    in_specs = (
        P("wa", None, "pb"),
        P("wa", None, "pb"),
        P("wa", "pb"),
        P("pb", "wa", None),
        P("pb", None),
    )
    return jax.shard_map(
        shards, mesh=mesh, in_specs=in_specs, out_specs=P("wa", "pb"), check_vma=False
    )
```
